32 devices in a mesh: seq: 8 (over z, x), tp: 4 (over y, core).
Axes of the slice: x: 2, y: 2, z: 4, core: 2. Of those that a mesh axis runs over, the one named last changes fastest.
Arguments:
- tokens_in: bfloat16 [4, 16, 1024], replicated, may hold values from -6 to 6
- key_cache: bfloat16 [16, 2048, 1024], P(None, 'seq', 'tp'), may hold values from -6 to 6
- value_cache: bfloat16 [16, 2048, 1024], P(None, 'seq', 'tp'), may hold values from -6 to 6
- cache_len: int32 [16], replicated, may hold values from 1 to 2048, as said below
- bucket_table: int32 [2052], replicated, may hold values from 0 to 31, as said below
- rel_bias: float32 [32, 16], P(None, 'tp'), may hold values from -4 to 283
- attn_gain: float32 [1024], replicated, may hold values from 0.1 to 1.9
- moe_gain: float32 [1024], replicated, may hold values from 0.1 to 1.9
- w_qkv: bfloat16 [3, 1024, 1024], P(None, None, 'tp'), may hold values from -0.1875 to 0.1875
- w_out: bfloat16 [1024, 1024], P('tp'), may hold values from -0.1875 to 0.1875
- router: bfloat16 [1024, 16], replicated, may hold values from -0.1875 to 0.1875
- expert_choice: int32 [4, 16, 2], replicated, may hold values from 0 to 15, all different within a row
- w_gate_up: bfloat16 [2, 45056, 1024], P(None, ('seq', 'tp')), may hold values from -0.1875 to 0.1875
- w_down: bfloat16 [45056, 1024], P(('seq', 'tp')), may hold values from -0.109375 to 0.109375
Outputs:
- layer_out: bfloat16 [4, 16, 1024], replicated
The draws below stay inside these ranges and needn't reach their ends.
Inputs may be any that keep to these rules, and one draw needn't show every extreme that they name: Request r's cache holds its positions 0 to cache_len[r] - 1; some request holds exactly 2048. `bucket_table`: non-decreasing in the distance, 0 at distance 0. `expert_choice`: the 2 experts of a token differ.
All inputs are finite; a program needn't handle non-finite values.
Results may differ from the reference program's by a relative error of at most 0.012.
Values sent between devices are 32-bit elements; how exact they have to be, the bound alone decides.
No kernel may reach another device: no remote copies, remote signals or barrier semaphores. Data moves between devices by JAX's collectives and lax.ppermute only.
A program may use at most 64 MiB of HBM per device.

```python
import jax
import jax.numpy as jnp
from jax import lax

D = 1024
HEADS = 16
HEAD_DIM = 64
EXPERTS = 16
FF = 2816
TOP = 2
NB = 32
STEPS = 4
REQ = 16
LMAX = 2048


def draw_cache_len(key, part):
    first_key, second_key = jax.random.split(key)
    lengths = jax.random.randint(first_key, (REQ,), 1, LMAX + 1, dtype=jnp.int32)
    longest = jax.random.randint(second_key, (), 0, REQ, dtype=jnp.int32)
    return lengths.at[longest].set(LMAX)


def draw_bucket_table(key, part):
    table_len = LMAX + STEPS
    marked = jax.random.permutation(key, table_len - 1)[:NB - 1] + 1
    marks = jnp.zeros((table_len,), jnp.int32).at[marked].set(1)
    return jnp.cumsum(marks).astype(jnp.int32)


def draw_rel_bias(key, part):
    first_key = jax.random.fold_in(key, 0)
    return jnp.clip(jax.random.normal(first_key, (NB, HEADS), jnp.float32), -4.0, 4.0)


def level_of(key, shape, cuts, least, high):
    level, own = 1.0, jax.random.fold_in(key, 6)
    for position, blocks in cuts:
        steps = jnp.exp(jax.random.uniform(jax.random.fold_in(own, position), (blocks,), jnp.float32, least / len(cuts), high / len(cuts)))
        level = level * jnp.repeat(steps, shape[position] // blocks).reshape([-1 if axis == position else 1 for axis in range(len(shape))])
    return level


def choose_distinct(stream_key, rows, number_of, top, lift):
    order = jax.random.permutation(jax.random.fold_in(stream_key, 1), number_of)
    favour = order
    for power in range(3):
        favour = favour * favour // number_of
    favour = favour * lift // number_of
    lots = jax.random.randint(jax.random.fold_in(stream_key, 2), (rows, number_of), 0, 4096) + favour
    holders = jax.random.permutation(jax.random.fold_in(stream_key, 3), rows)[jnp.arange(number_of) % rows]
    lots = jnp.where(jnp.arange(rows)[:, None] == holders[None, :], 1 << 14, lots)
    priority = lots * number_of + jnp.arange(number_of)
    return lax.top_k(priority.astype(jnp.int32), top)[1].astype(jnp.int32)


def bell_draw(key, shape, width, bound, cuts=(), kind=jnp.bfloat16):
    entries = width * jax.random.normal(key, shape, jnp.float32)
    if cuts:
        entries = entries * level_of(key, shape, cuts, -0.22, 0.18)
    return jnp.clip(entries, -bound, bound).astype(kind)


def setup_inputs(seed: int = 0) -> dict:
    splits = jax.random.split(jax.random.key(seed), 15)
    tokens_in = bell_draw(splits[0], (STEPS, REQ, D), 1.0, 6.0)
    key_cache = bell_draw(splits[1], (REQ, LMAX, HEADS * HEAD_DIM), 1.0, 6.0, ((1, 8), (2, 4)))
    value_cache = bell_draw(splits[2], (REQ, LMAX, HEADS * HEAD_DIM), 1.0, 6.0, ((1, 8), (2, 4)))
    cache_len = draw_cache_len(jax.random.fold_in(splits[14], 71), 0)
    bucket_table = draw_bucket_table(jax.random.fold_in(splits[14], 71), 0)
    rel_bias = draw_rel_bias(jax.random.fold_in(splits[14], 71), 0)
    attn_gain = jnp.clip(1.0 + 0.18 * jax.random.normal(splits[6], (D,), jnp.float32), 0.1, 1.9)
    moe_gain = jnp.clip(1.0 + 0.18 * jax.random.normal(splits[7], (D,), jnp.float32), 0.1, 1.9)
    w_qkv = bell_draw(splits[8], (3, D, HEADS * HEAD_DIM), D ** -0.5, 0.1875, ((2, 4),))
    w_out = bell_draw(splits[9], (HEADS * HEAD_DIM, D), (HEADS * HEAD_DIM) ** -0.5, 0.1875, ((0, 4),))
    router = bell_draw(splits[10], (D, EXPERTS), D ** -0.5, 0.1875)
    expert_choice = choose_distinct(splits[11], STEPS * REQ, EXPERTS, TOP, 1024).reshape((STEPS, REQ, TOP))
    w_gate_up = bell_draw(splits[12], (2, EXPERTS * FF, D), D ** -0.5, 0.1875, ((1, 32),))
    w_down = bell_draw(splits[13], (EXPERTS * FF, D), FF ** -0.5, 0.109375, ((0, 32),))
    return dict(tokens_in=tokens_in, key_cache=key_cache, value_cache=value_cache, cache_len=cache_len, bucket_table=bucket_table, rel_bias=rel_bias, attn_gain=attn_gain, moe_gain=moe_gain, w_qkv=w_qkv, w_out=w_out, router=router, expert_choice=expert_choice, w_gate_up=w_gate_up, w_down=w_down)


NEG = -1e+30
EPS = 1e-06

def rms_scale(values, gain_vec):
    return values * lax.rsqrt(lax.optimization_barrier(jnp.mean(values * values, axis=-1, keepdims=True)) + EPS) * gain_vec

def reference(tokens_in, key_cache, value_cache, cache_len, bucket_table, rel_bias, attn_gain, moe_gain, w_qkv, w_out, router, expert_choice, w_gate_up, w_down):
    normed = rms_scale(tokens_in.astype(jnp.float32), attn_gain).astype(jnp.bfloat16)
    projected = jnp.einsum('srd,kdf->ksrf', normed.astype(jnp.float32), w_qkv.astype(jnp.float32)).astype(jnp.bfloat16)
    head_shape = (STEPS, REQ, HEADS, HEAD_DIM)
    queries = projected[0].reshape(head_shape).astype(jnp.float32)
    fresh_keys = jnp.swapaxes(projected[1].reshape(head_shape).astype(jnp.float32), 0, 1)
    fresh_values = jnp.swapaxes(projected[2].reshape(head_shape).astype(jnp.float32), 0, 1)
    keys_heads = key_cache.reshape(REQ, LMAX, HEADS, HEAD_DIM)
    values_heads = value_cache.reshape(REQ, LMAX, HEADS, HEAD_DIM)
    positions = jnp.arange(LMAX, dtype=jnp.int32)
    recent = jnp.arange(STEPS, dtype=jnp.int32)
    table_len = LMAX + STEPS
    outputs = []
    for step_num in range(STEPS):

        def attend(pieces):
            query_row, keys_one, values_one, length, fresh_key_rows, fresh_value_rows = pieces
            cache_scores = jnp.einsum('hd,lhd->hl', query_row, keys_one.astype(jnp.float32))
            distance = length + step_num - positions
            cache_bias = rel_bias[bucket_table[jnp.clip(distance, 0, table_len - 1)]]
            live_one = positions < length
            cache_scores = jnp.where(live_one[None, :], cache_scores + cache_bias.T, NEG)
            new_bias = rel_bias[bucket_table[jnp.clip(step_num - recent, 0, table_len - 1)]]
            new_scores = jnp.einsum('hd,jhd->hj', query_row, fresh_key_rows) + new_bias.T
            new_live = recent <= step_num
            new_scores = jnp.where(new_live[None, :], new_scores, NEG)
            scores = jnp.concatenate([cache_scores, new_scores], axis=1)
            usable = jnp.concatenate([live_one, new_live])[None, :]
            row_peak = lax.optimization_barrier(jnp.max(scores, axis=-1, keepdims=True))
            weights = jnp.where(usable, jnp.exp(scores - row_peak), 0.0)
            values_all = jnp.concatenate([values_one.astype(jnp.float32), fresh_value_rows], axis=0)
            return jnp.einsum('hl,lhd->hd', weights, values_all) / lax.optimization_barrier(jnp.sum(weights, axis=-1))[:, None]
        attended = lax.map(attend, (queries[step_num], keys_heads, values_heads, cache_len, fresh_keys, fresh_values))
        attended = attended.reshape(REQ, HEADS * HEAD_DIM).astype(jnp.bfloat16)
        mid = tokens_in[step_num].astype(jnp.float32) + jnp.dot(attended, w_out, preferred_element_type=jnp.float32)
        moe_in = rms_scale(mid, moe_gain).astype(jnp.bfloat16)
        logits = jnp.dot(moe_in, router, preferred_element_type=jnp.float32)
        chosen = jnp.take_along_axis(logits, expert_choice[step_num], axis=1)
        leading = jax.nn.sigmoid(chosen[:, 0] - chosen[:, 1])
        gate_pair = jnp.stack([leading, 1.0 - leading], axis=-1)
        picked = expert_choice[step_num][..., None] == jnp.arange(EXPERTS, dtype=jnp.int32)
        per_expert = lax.optimization_barrier(jnp.sum(jnp.where(picked, gate_pair[..., None], 0.0), axis=1))

        def expert_step(running, expert_idx):
            gate_rows = lax.dynamic_slice_in_dim(w_gate_up[0], expert_idx * FF, FF, 0)
            up_rows = lax.dynamic_slice_in_dim(w_gate_up[1], expert_idx * FF, FF, 0)
            down_rows = lax.dynamic_slice_in_dim(w_down, expert_idx * FF, FF, 0)
            gate_part = jnp.dot(moe_in, gate_rows.T, preferred_element_type=jnp.float32)
            up_part = jnp.dot(moe_in, up_rows.T, preferred_element_type=jnp.float32)
            coef = lax.dynamic_slice_in_dim(per_expert, expert_idx, 1, 1)
            hidden = (jax.nn.gelu(gate_part, approximate=True) * up_part * coef).astype(jnp.bfloat16)
            return (running + jnp.dot(hidden, down_rows, preferred_element_type=jnp.float32), None)
        mixture, _ = lax.scan(expert_step, jnp.zeros((REQ, D), jnp.float32), jnp.arange(EXPERTS, dtype=jnp.int32))
        outputs.append((mid + mixture).astype(jnp.bfloat16))
    return jnp.stack(outputs)
```

```python
import jax
import jax.numpy as jnp
from jax import lax
from jax.sharding import PartitionSpec as P

HEAD_DIM = 64
FF = 2816


NEG = -1e30
EPS = 1e-06


def rms_scale(values, gain_vec):
    return values * lax.rsqrt(jnp.mean(values * values, axis=-1, keepdims=True) + EPS) * gain_vec


def on_device(
    tokens_in,
    key_cache,
    value_cache,
    cache_len,
    bucket_table,
    rel_bias,
    attn_gain,
    moe_gain,
    w_qkv,
    w_out,
    router,
    expert_choice,
    w_gate_up,
    w_down,
):
    steps_all, requests, model_width = tokens_in.shape
    cache_rows = key_cache.shape[1]
    heads_local = key_cache.shape[2] // HEAD_DIM
    table_len = bucket_table.shape[0]
    num_buckets = rel_bias.shape[0]
    num_experts = router.shape[1]
    hidden_local = w_down.shape[0]
    bucket_ids = jnp.arange(num_buckets, dtype=jnp.int32)

    def bias_lookup(buckets, pattern):
        onehot = (buckets[..., None] == bucket_ids).astype(jnp.float32)
        return jnp.einsum(pattern, onehot, rel_bias, precision=lax.Precision.HIGHEST)

    normed = rms_scale(tokens_in.astype(jnp.float32), attn_gain).astype(jnp.bfloat16)
    projected = jnp.einsum(
        "srd,kdf->ksrf", normed, w_qkv, preferred_element_type=jnp.float32
    ).astype(jnp.bfloat16)
    head_shape = (steps_all, requests, heads_local, HEAD_DIM)
    queries = projected[0].reshape(head_shape)
    fresh_keys = projected[1].reshape(head_shape)
    fresh_values = projected[2].reshape(head_shape)
    keys_heads = key_cache.reshape(requests, cache_rows, heads_local, HEAD_DIM)
    values_heads = value_cache.reshape(requests, cache_rows, heads_local, HEAD_DIM)
    positions = lax.axis_index("seq") * cache_rows + jnp.arange(cache_rows, dtype=jnp.int32)
    live_rows = positions[None, :] < cache_len[:, None]

    def cache_part(query_blk, step_ids, keys_blk, vals_blk, lens_blk, live_blk):
        scores = jnp.einsum(
            "srhd,rchd->srhc", query_blk, keys_blk, preferred_element_type=jnp.float32
        )
        distance = lens_blk[None, :, None] + step_ids[:, None, None] - positions[None, None, :]
        buckets = jnp.take(bucket_table, jnp.clip(distance, 0, table_len - 1))
        scores = scores + bias_lookup(buckets, "srcb,bh->srhc")
        usable = live_blk[None, :, None, :]
        scores = jnp.where(usable, scores, NEG)
        maxima = jnp.max(scores, axis=-1)
        weights = jnp.where(usable, jnp.exp(scores - maxima[..., None]), 0.0)
        summed = jnp.einsum(
            "srhc,rchd->srhd", weights, vals_blk, preferred_element_type=jnp.float32
        )
        return (maxima, jnp.sum(weights, axis=-1), summed)

    def attend_cache(query_blk, step_ids):
        return cache_part(query_blk, step_ids, keys_heads, values_heads, cache_len, live_rows)

    def merge_cache(maxima, totals, summed):
        overall = lax.pmax(maxima, "seq")
        factor = jnp.exp(maxima - overall)
        totals, summed = lax.psum((totals * factor, summed * factor[..., None]), "seq")
        return (overall, totals, summed)

    def attend_recent(query_blk, step_ids):
        scores = jnp.einsum(
            "srhd,jrhd->srhj", query_blk, fresh_keys, preferred_element_type=jnp.float32
        )
        distance = step_ids[:, None] - jnp.arange(steps_all, dtype=jnp.int32)[None, :]
        buckets = jnp.take(bucket_table, jnp.clip(distance, 0, table_len - 1))
        scores = scores + bias_lookup(buckets, "sjb,bh->shj")[:, None]
        usable = (distance >= 0)[:, None, None, :]
        scores = jnp.where(usable, scores, NEG)
        maxima = jnp.max(scores, axis=-1)
        weights = jnp.where(usable, jnp.exp(scores - maxima[..., None]), 0.0)
        summed = jnp.einsum(
            "srhj,jrhd->srhd", weights, fresh_values, preferred_element_type=jnp.float32
        )
        return (maxima, jnp.sum(weights, axis=-1), summed)

    first_col = (lax.axis_index("seq") * lax.axis_size("tp") + lax.axis_index("tp")) * hidden_local
    col_expert = (first_col + jnp.arange(hidden_local, dtype=jnp.int32)) // FF
    owner = (col_expert[None, :] == jnp.arange(num_experts, dtype=jnp.int32)[:, None]).astype(
        jnp.float32
    )

    def layer(start, step_count):
        step_ids = jnp.arange(start, start + step_count, dtype=jnp.int32)
        query_blk = queries[start : start + step_count]
        cache_max, cache_tot, cache_sum = merge_cache(*attend_cache(query_blk, step_ids))
        new_max, new_tot, new_sum = attend_recent(query_blk, step_ids)
        joint = jnp.maximum(cache_max, new_max)
        scale_cache = jnp.exp(cache_max - joint)
        scale_new = jnp.exp(new_max - joint)
        totals = cache_tot * scale_cache + new_tot * scale_new
        summed = cache_sum * scale_cache[..., None] + new_sum * scale_new[..., None]
        attended = (
            (summed / totals[..., None])
            .reshape(step_count, requests, heads_local * HEAD_DIM)
            .astype(jnp.bfloat16)
        )
        partial_value = jnp.einsum(
            "srf,fd->srd", attended, w_out, preferred_element_type=jnp.float32
        )
        mid = tokens_in[start : start + step_count].astype(jnp.float32) + lax.psum(
            partial_value, "tp"
        )
        moe_in = rms_scale(mid, moe_gain).astype(jnp.bfloat16)
        logits = jnp.einsum("srd,de->sre", moe_in, router, preferred_element_type=jnp.float32)
        picked = expert_choice[start : start + step_count][..., None] == jnp.arange(
            num_experts, dtype=jnp.int32
        )
        chosen = jnp.sum(jnp.where(picked, logits[:, :, None, :], 0.0), axis=-1)
        leading = jax.nn.sigmoid(chosen[..., 0] - chosen[..., 1])
        gate_pair = jnp.stack([leading, 1.0 - leading], axis=-1)
        per_expert = jnp.sum(jnp.where(picked, gate_pair[..., None], 0.0), axis=2)
        coef = jnp.einsum("sre,ef->srf", per_expert, owner, precision=lax.Precision.HIGHEST)
        gate_up = jnp.einsum("srd,kfd->ksrf", moe_in, w_gate_up, preferred_element_type=jnp.float32)
        hidden = (jax.nn.gelu(gate_up[0], approximate=True) * gate_up[1] * coef).astype(
            jnp.bfloat16
        )
        expert_part = jnp.einsum("srf,fd->srd", hidden, w_down, preferred_element_type=jnp.float32)
        mixture = lax.psum(expert_part, ("seq", "tp"))
        return (mid + mixture).astype(jnp.bfloat16)

    return layer(0, steps_all)


def solution(mesh):
    return jax.shard_map(
        on_device,
        mesh=mesh,
        in_specs=(
            P(),
            P(None, "seq", "tp"),
            P(None, "seq", "tp"),
            P(),
            P(),
            P(None, "tp"),
            P(),
            P(),
            P(None, None, "tp"),
            P("tp", None),
            P(),
            P(),
            P(None, ("seq", "tp"), None),
            P(("seq", "tp"), None),
        ),
        out_specs=P(),
        check_vma=False,
    )
```

```python
import jax
import jax.numpy as jnp
from jax import lax
from jax.sharding import PartitionSpec as P

HEAD_DIM = 64
FF = 2816


NEG = -1e30
EPS = 1e-06


def rms_scale(values, gain_vec):
    return values * lax.rsqrt(jnp.mean(values * values, axis=-1, keepdims=True) + EPS) * gain_vec


def swap(value, axis, bit):
    size = lax.axis_size(axis)
    return lax.ppermute(value, axis, [(i, i ^ bit) for i in range(size)])


def bits_of(axis):
    size = lax.axis_size(axis)
    assert size & (size - 1) == 0
    return [1 << k for k in range(size.bit_length() - 1)]


def sum_over(make_half, rows, swaps):
    (axis, bit), others = swaps[0], swaps[1:]
    side = (lax.axis_index(axis) // bit) % 2
    given = swap(make_half(1 - side), axis, bit)
    half = make_half(side) + given
    for other_axis, other_bit in others:
        half = half + swap(half, other_axis, other_bit)
    back = swap(half, axis, bit)
    return jnp.where(side == 0, jnp.concatenate([half, back]), jnp.concatenate([back, half]))


def on_device(
    tokens_in,
    key_cache,
    value_cache,
    cache_len,
    bucket_table,
    rel_bias,
    attn_gain,
    moe_gain,
    w_qkv,
    w_out,
    router,
    expert_choice,
    w_gate_up,
    w_down,
):
    steps, requests, width = tokens_in.shape
    tokens = steps * requests
    cache_rows = key_cache.shape[1]
    features = key_cache.shape[2]
    heads = features // HEAD_DIM
    num_buckets = rel_bias.shape[0]
    num_experts = router.shape[1]
    hidden_local = w_down.shape[0]

    starts = jnp.sum(
        (bucket_table[None, :] < jnp.arange(num_buckets, dtype=jnp.int32)[:, None]).astype(jnp.int32), axis=1
    )

    def bias_of(distance):
        bias = jnp.broadcast_to(rel_bias[0], distance.shape + (heads,))
        for b in range(1, num_buckets):
            bias = jnp.where((distance >= starts[b])[..., None], rel_bias[b], bias)
        return bias

    flat_in = tokens_in.reshape(tokens, width).astype(jnp.float32)
    normed = rms_scale(flat_in, attn_gain).astype(jnp.bfloat16)
    projected = jnp.einsum("td,kdf->ktf", normed, w_qkv, preferred_element_type=jnp.float32).astype(jnp.bfloat16)
    head_shape = (steps, requests, heads, HEAD_DIM)
    queries = projected[0].reshape(head_shape)
    fresh_keys = projected[1].reshape(head_shape)
    fresh_values = projected[2].reshape(head_shape)
    keys_heads = key_cache.reshape(requests, cache_rows, heads, HEAD_DIM)
    values_heads = value_cache.reshape(requests, cache_rows, heads, HEAD_DIM)
    positions = lax.axis_index("seq") * cache_rows + jnp.arange(cache_rows, dtype=jnp.int32)
    step_ids = jnp.arange(steps, dtype=jnp.int32)

    scores = jnp.einsum("srhd,rchd->rshc", queries, keys_heads, preferred_element_type=jnp.float32)
    distance = cache_len[:, None, None] + step_ids[None, :, None] - positions[None, None, :]
    bias = jnp.broadcast_to(rel_bias[0][None, None, :, None], scores.shape)
    for b in range(1, num_buckets):
        bias = jnp.where((distance >= starts[b])[:, :, None, :], rel_bias[b][None, None, :, None], bias)
    usable = (positions[None, :] < cache_len[:, None])[:, None, None, :]
    scores = jnp.where(usable, scores + bias, NEG)
    maxima = jnp.max(scores, axis=-1)
    weights = jnp.where(usable, jnp.exp(scores - maxima[..., None]), 0.0)
    totals = jnp.sum(weights, axis=-1)
    summed = jnp.einsum(
        "rshc,rchd->rshd", weights.astype(jnp.bfloat16), values_heads, preferred_element_type=jnp.float32
    )

    def spread(stat):
        return jnp.broadcast_to(stat[..., None], stat.shape + (HEAD_DIM,))

    stats = jnp.concatenate([maxima.reshape(tokens, heads), totals.reshape(tokens, heads)], axis=1)
    stats = jnp.pad(stats, ((0, 0), (0, 128 - 2 * heads)))
    packed = jnp.concatenate([summed.reshape(tokens, features), stats], axis=1)

    def unpack(packed):
        sums = packed[:, :features].reshape(tokens, heads, HEAD_DIM)
        return packed[:, features : features + heads], packed[:, features + heads : features + 2 * heads], sums

    def merge(one, two):
        (max_one, tot_one, sum_one), (max_two, tot_two, sum_two) = one, two
        top = jnp.maximum(max_one, max_two)
        scale_one, scale_two = jnp.exp(max_one - top), jnp.exp(max_two - top)
        return (
            top,
            tot_one * scale_one + tot_two * scale_two,
            sum_one * spread(scale_one) + sum_two * spread(scale_two),
        )

    for bit in bits_of("seq"):
        top, tot, sums = merge(unpack(packed), unpack(swap(packed, "seq", bit)))
        packed = jnp.concatenate(
            [sums.reshape(tokens, features), jnp.pad(jnp.concatenate([top, tot], 1), ((0, 0), (0, 128 - 2 * heads)))], 1
        )

    new_scores = jnp.einsum("srhd,jrhd->rshj", queries, fresh_keys, preferred_element_type=jnp.float32)
    new_distance = step_ids[:, None] - step_ids[None, :]
    new_scores = new_scores + bias_of(new_distance).transpose(0, 2, 1)[None]
    new_usable = (new_distance >= 0)[None, :, None, :]
    new_scores = jnp.where(new_usable, new_scores, NEG)
    new_max = jnp.max(new_scores, axis=-1)
    new_weights = jnp.where(new_usable, jnp.exp(new_scores - new_max[..., None]), 0.0)
    new_sum = jnp.einsum("rshj,jrhd->rshd", new_weights, fresh_values, preferred_element_type=jnp.float32)
    new_part = (
        new_max.reshape(tokens, heads),
        jnp.sum(new_weights, axis=-1).reshape(tokens, heads),
        new_sum.reshape(tokens, heads, HEAD_DIM),
    )
    _, totals, summed = merge(unpack(packed), new_part)
    attended = (summed / spread(totals)).reshape(requests, steps, features).astype(jnp.bfloat16)
    attended = attended.transpose(1, 0, 2).reshape(tokens, features)

    half_rows = tokens // 2
    tp_swaps = [("tp", bit) for bit in bits_of("tp")]
    all_swaps = tp_swaps + [("seq", bit) for bit in bits_of("seq")]

    def rows_of(value, side):
        return lax.dynamic_slice_in_dim(value, side * half_rows, half_rows, 0)

    mid = flat_in + sum_over(
        lambda side: jnp.dot(rows_of(attended, side), w_out, preferred_element_type=jnp.float32), tokens, tp_swaps
    )
    moe_in = rms_scale(mid, moe_gain).astype(jnp.bfloat16)
    logits = jnp.dot(moe_in, router, preferred_element_type=jnp.float32)
    choice = expert_choice.reshape(tokens, -1)
    picked = choice[..., None] == jnp.arange(num_experts, dtype=jnp.int32)
    chosen = jnp.sum(jnp.where(picked, logits[:, None, :], 0.0), axis=-1)
    leading = jax.nn.sigmoid(chosen[:, 0] - chosen[:, 1])
    gate_pair = jnp.stack([leading, 1.0 - leading], axis=-1)
    device = lax.axis_index("seq") * lax.axis_size("tp") + lax.axis_index("tp")
    col_expert = (device * hidden_local + jnp.arange(hidden_local, dtype=jnp.int32)) // FF
    coef = jnp.where(choice[:, 0:1] == col_expert[None, :], gate_pair[:, 0:1], 0.0)
    coef = jnp.where(choice[:, 1:2] == col_expert[None, :], gate_pair[:, 1:2], coef)
    gate_up = jnp.einsum("td,kfd->ktf", moe_in, w_gate_up, preferred_element_type=jnp.float32)
    hidden = (jax.nn.gelu(gate_up[0], approximate=True) * gate_up[1] * coef).astype(jnp.bfloat16)
    mixture = sum_over(
        lambda side: jnp.dot(rows_of(hidden, side), w_down, preferred_element_type=jnp.float32), tokens, all_swaps
    )
    return (mid + mixture).astype(jnp.bfloat16).reshape(steps, requests, width)


def solution(mesh):
    return jax.shard_map(
        on_device,
        mesh=mesh,
        in_specs=(
            P(),
            P(None, "seq", "tp"),
            P(None, "seq", "tp"),
            P(),
            P(),
            P(None, "tp"),
            P(),
            P(),
            P(None, None, "tp"),
            P("tp", None),
            P(),
            P(),
            P(None, ("seq", "tp"), None),
            P(("seq", "tp"), None),
        ),
        out_specs=P(),
        check_vma=False,
    )
```

```python
import functools

import jax
import jax.numpy as jnp
from jax import lax
from jax.experimental import pallas as pl
from jax.experimental.pallas import tpu as pltpu
from jax.sharding import PartitionSpec as P

HEAD_DIM = 64
FF = 2816
LANES = 128
NEG = -1e30
EPS = 1e-06
F32 = jnp.float32
BF16 = jnp.bfloat16
VMEM = pl.BlockSpec(memory_space=pltpu.VMEM)
SMEM = pl.BlockSpec(memory_space=pltpu.SMEM)
ANY = pl.BlockSpec(memory_space=pl.ANY)
NT = (((1,), (1,)), ((), ()))


def dot(one, two):
    return jnp.dot(one, two, preferred_element_type=F32)


def dot_nt(one, two):
    return lax.dot_general(one, two, NT, preferred_element_type=F32)


def iota(shape, dim):
    return lax.broadcasted_iota(jnp.int32, shape, dim)


def rms_scale(values, gain_vec):
    return values * lax.rsqrt(jnp.mean(values * values, axis=-1, keepdims=True) + EPS) * gain_vec


def attend_kernel(
    steps, requests, heads, len_ref, tokens_ref, gain_ref, table_ref, rel_ref, w_hbm, k_hbm, v_hbm,
    out_ref, w_buf, k_buf, v_buf, bias_buf, score_buf, weight_buf, start_buf, step_buf, w_sem, k_sem, v_sem,
):
    tokens = steps * requests
    group = steps * heads
    rows = requests * group
    buckets = rel_ref.shape[1]
    cache_rows, features = k_buf.shape[1:]
    w_copies = [pltpu.make_async_copy(w_hbm.at[k], w_buf.at[k], w_sem.at[k]) for k in range(3)]
    k_copies = [pltpu.make_async_copy(k_hbm.at[r], k_buf.at[r], k_sem.at[r]) for r in range(requests)]
    v_copies = [pltpu.make_async_copy(v_hbm.at[r], v_buf.at[r], v_sem.at[r]) for r in range(requests)]
    for copy in w_copies + k_copies + v_copies:
        copy.start()

    seq = lax.axis_index("seq")
    base = seq * cache_rows

    table = table_ref[...]
    below = jnp.where(table < iota((buckets, table.shape[1]), 0), 1.0, 0.0)
    starts = jnp.sum(below, axis=1, keepdims=True).astype(jnp.int32)
    start_buf[...] = jnp.broadcast_to(starts, (buckets, LANES))

    group_head = iota((group, buckets), 0) // steps
    level = jnp.zeros((group, buckets), F32)
    for h in range(heads):
        level = jnp.where(group_head == h, rel_ref[h : h + 1, :], level)
    for b in range(buckets):
        step_buf[b] = jnp.broadcast_to(level[:, b : b + 1], (group, LANES))

    def bias_of(distance):
        parts = []
        for c in range(0, distance.shape[1], LANES):
            piece = distance[:, c : c + LANES]
            bias = step_buf[0][:, : piece.shape[1]]
            for b in range(1, buckets):
                bias = jnp.where(
                    piece >= start_buf[b : b + 1, : piece.shape[1]], step_buf[b][:, : piece.shape[1]], bias
                )
            parts.append(bias)
        return parts

    group_step = iota((group, cache_rows), 0) % steps
    offset = group_step - iota((group, cache_rows), 1) - base

    def fill_bias(r, carry):
        length = len_ref[r]
        distance = offset + length
        live = distance > group_step
        parts = bias_of(distance)
        for c, bias in enumerate(parts):
            cols = slice(c * LANES, c * LANES + bias.shape[1])
            bias_buf[pl.ds(pl.multiple_of(r * group, group), group), cols] = jnp.where(live[:, cols], bias, NEG)
        return carry

    lax.fori_loop(0, requests, fill_bias, 0)

    x = tokens_ref[...].astype(F32)
    normed = rms_scale(x, gain_ref[...]).astype(BF16)
    projected = []
    for k in range(3):
        w_copies[k].wait()
        projected.append(dot(normed, w_buf[k]).astype(BF16))
    queries, fresh_keys, fresh_values = projected

    row = iota((rows, tokens), 0)
    source = (row % steps) * requests + row // group
    pick = jnp.where(source == iota((rows, tokens), 1), 1.0, 0.0).astype(BF16)
    own_head = (iota((rows, features), 0) // steps) % heads == iota((rows, features), 1) // HEAD_DIM
    spread = jnp.where(own_head, dot(pick, queries), 0.0).astype(BF16)

    column = iota((rows, tokens), 1)
    key_step, key_request = column // requests, column % requests
    ahead = row % steps - key_step
    fresh_live = jnp.logical_and(jnp.logical_and(ahead >= 0, key_request == row // group), seq == 0)
    group_ahead = iota((group, tokens), 0) % steps - iota((group, tokens), 1) // requests
    fresh_bias = bias_of(group_ahead)[0]
    fresh_bias = jnp.concatenate([fresh_bias] * requests, axis=0)
    fresh_scores = jnp.where(fresh_live, dot_nt(spread, fresh_keys) + fresh_bias, NEG)

    for r in range(requests):
        at = slice(r * group, (r + 1) * group)
        k_copies[r].wait()
        score_buf[at, :] = dot_nt(spread[at], k_buf[r])
    scores = score_buf[...] + bias_buf[...]
    top = jnp.maximum(jnp.max(scores, axis=1, keepdims=True), jnp.max(fresh_scores, axis=1, keepdims=True))
    weights = jnp.where(scores > 0.5 * NEG, jnp.exp(scores - top), 0.0)
    fresh_weights = jnp.where(fresh_live, jnp.exp(fresh_scores - top), 0.0)
    total = jnp.sum(weights, axis=1, keepdims=True) + jnp.sum(fresh_weights, axis=1, keepdims=True)
    weight_buf[...] = weights.astype(BF16)
    score_buf[...] = dot(fresh_weights.astype(BF16), fresh_values)
    for r in range(requests):
        at = slice(r * group, (r + 1) * group)
        v_copies[r].wait()
        score_buf[at, :] += dot(weight_buf[at, :], v_buf[r])

    sums = jnp.where(own_head, score_buf[...], 0.0)
    lane = iota((rows, LANES), 1)
    head = (iota((rows, LANES), 0) // steps) % heads
    stats = jnp.where(lane == head, top, jnp.where(lane == heads + head, total, 0.0))
    first = iota((8, 1), 0) < steps
    for values, cols in ((sums, slice(0, features)), (stats, slice(features, features + LANES))):
        for pair in range(requests // 2):
            folded = []
            for r in (2 * pair, 2 * pair + 1):
                part = values[r * group : r * group + 8] + values[r * group + 8 : r * group + 16]
                folded.append(part + pltpu.roll(part, steps, 0))
            out_ref[8 * pair : 8 * pair + 8, cols] = jnp.where(first, folded[0], folded[1])


def widen(stats, first, features):
    heads = features // HEAD_DIM
    lane_head = iota((stats.shape[0], features), 1) // HEAD_DIM
    wide = jnp.broadcast_to(stats[:, first : first + 1], lane_head.shape)
    for h in range(1, heads):
        wide = jnp.where(lane_head == h, stats[:, first + h : first + h + 1], wide)
    return wide


def merged(features, one_ref, two_ref):
    heads = features // HEAD_DIM
    one, two = one_ref[:, features:], two_ref[:, features:]
    top = jnp.maximum(one, two)
    scale_one, scale_two = jnp.exp(one - top), jnp.exp(two - top)
    totals = one * pltpu.roll(scale_one, heads, 1) + two * pltpu.roll(scale_two, heads, 1)
    sums = one_ref[:, :features] * widen(scale_one, 0, features) + two_ref[:, :features] * widen(scale_two, 0, features)
    return sums, jnp.where(iota(top.shape, 1) < heads, top, totals)


def merge_kernel(features, one_ref, two_ref, out_ref):
    sums, stats = merged(features, one_ref, two_ref)
    out_ref[:, :features] = sums
    out_ref[:, features:] = stats


def store_halves(value, bit, keep_ref, give_ref):
    half = value.shape[0] // 2
    low = lax.axis_index("tp") // bit % 2 == 0
    keep_ref[...] = jnp.where(low, value[:half], value[half:])
    give_ref[...] = jnp.where(low, value[half:], value[:half])


def project_kernel(steps, requests, features, one_ref, two_ref, w_ref, keep_ref, give_ref):
    sums, stats = merged(features, one_ref, two_ref)
    attended = (sums / widen(stats, features // HEAD_DIM, features)).astype(BF16)
    tokens = steps * requests
    row = iota((tokens, tokens), 0)
    source = (row % requests) * steps + row // requests
    order = jnp.where(source == iota((tokens, tokens), 1), 1.0, 0.0).astype(BF16)
    attended = dot(order, attended).astype(BF16)
    store_halves(dot(attended, w_ref[...]), 1, keep_ref, give_ref)


def chunks_of(total, size):
    return [(at, min(size, total - at)) for at in range(0, total, size)]


def expert_kernel(
    half_ref, back_ref, tokens_ref, gain_ref, router_ref, choice_ref, up_hbm, down_hbm,
    mid_ref, keep_ref, give_ref, up_buf, down_buf, up_sem, down_sem,
):
    hidden_local = down_buf.shape[0]
    chunks = chunks_of(hidden_local, 256)
    copies = []
    for i, (at, size) in enumerate(chunks):
        at = pl.ds(at, size)
        copies.append(
            [pltpu.make_async_copy(up_hbm.at[k, at], up_buf.at[k, at], up_sem.at[k, i]) for k in range(2)]
            + [pltpu.make_async_copy(down_hbm.at[at], down_buf.at[at], down_sem.at[i])]
        )
        for copy in copies[-1]:
            copy.start()
    half = half_ref.shape[0]
    low = lax.axis_index("tp") % 2 == 0
    mine, other = half_ref[...], back_ref[...]
    mid_ref[:half] = tokens_ref[:half].astype(F32) + jnp.where(low, mine, other)
    mid_ref[half:] = tokens_ref[half:].astype(F32) + jnp.where(low, other, mine)
    moe_in = rms_scale(mid_ref[...], gain_ref[...]).astype(BF16)
    logits = dot_nt(moe_in, router_ref[...])
    expert = iota(logits.shape, 1)
    first_choice, second_choice = choice_ref[:, 0:1], choice_ref[:, 1:2]
    chosen = [
        jnp.sum(jnp.where(expert == pick, logits, 0.0), axis=1, keepdims=True) for pick in (first_choice, second_choice)
    ]
    first = 1.0 / (1.0 + jnp.exp(chosen[1] - chosen[0]))
    second = 1.0 - first
    device = lax.axis_index("seq") * lax.axis_size("tp") + lax.axis_index("tp")
    total = jnp.zeros(mid_ref.shape, F32)
    for (at, size), (gate_copy, up_copy, down_copy) in zip(chunks, copies):
        column_expert = (device * hidden_local + at + iota((mid_ref.shape[0], size), 1)) // FF
        coef = jnp.where(
            column_expert == first_choice, first, jnp.where(column_expert == second_choice, second, 0.0)
        )
        gate_copy.wait()
        gate = dot_nt(moe_in, up_buf[0, at : at + size, :])
        up_copy.wait()
        up = dot_nt(moe_in, up_buf[1, at : at + size, :])
        hidden = (jax.nn.gelu(gate, approximate=True) * up * coef).astype(BF16)
        down_copy.wait()
        total = total + dot(hidden, down_buf[at : at + size, :])
    store_halves(total, 1, keep_ref, give_ref)


def swap(value, axis, bit):
    return lax.ppermute(value, axis, [(i, i ^ bit) for i in range(lax.axis_size(axis))])


def bits_of(axis):
    size = lax.axis_size(axis)
    assert size & (size - 1) == 0
    return [1 << k for k in range(size.bit_length() - 1)]


def reduce_halves(keep, give, swaps):
    half = keep + swap(give, *swaps[0])
    for axis, bit in swaps[1:]:
        half = half + swap(half, axis, bit)
    return half, swap(half, *swaps[0])


def call(kernel, out_shape, in_specs, scratch=()):
    shapes = [jax.ShapeDtypeStruct(shape, dtype) for shape, dtype in out_shape]
    return pl.pallas_call(
        kernel,
        out_shape=shapes,
        in_specs=in_specs,
        out_specs=[VMEM] * len(shapes),
        scratch_shapes=list(scratch),
        compiler_params=pltpu.CompilerParams(vmem_limit_bytes=40 << 20),
    )


def on_device(
    tokens_in,
    key_cache,
    value_cache,
    cache_len,
    bucket_table,
    rel_bias,
    attn_gain,
    moe_gain,
    w_qkv,
    w_out,
    router,
    expert_choice,
    w_gate_up,
    w_down,
):
    steps, requests, width = tokens_in.shape
    tokens = steps * requests
    half = tokens // 2
    _, cache_rows, features = key_cache.shape
    heads = features // HEAD_DIM
    rows = tokens * heads
    buckets = rel_bias.shape[0]
    hidden_local = w_down.shape[0]
    packed_shape = (tokens, features + LANES)
    flat_in = tokens_in.reshape(tokens, width)
    dma = pltpu.SemaphoreType.DMA

    (packed,) = call(
        functools.partial(attend_kernel, steps, requests, heads),
        [(packed_shape, F32)],
        [SMEM, VMEM, VMEM, VMEM, VMEM, ANY, ANY, ANY],
        [
            pltpu.VMEM(w_qkv.shape, BF16),
            pltpu.VMEM(key_cache.shape, BF16),
            pltpu.VMEM(value_cache.shape, BF16),
            pltpu.VMEM((rows, cache_rows), F32),
            pltpu.VMEM((rows, cache_rows), F32),
            pltpu.VMEM((rows, cache_rows), BF16),
            pltpu.VMEM((buckets, LANES), jnp.int32),
            pltpu.VMEM((buckets, steps * heads, LANES), F32),
            dma((3,)),
            dma((requests,)),
            dma((requests,)),
        ],
    )(
        cache_len, flat_in, attn_gain[None], bucket_table[None], rel_bias.T, w_qkv, key_cache, value_cache
    )

    seq_bits = bits_of("seq")
    for bit in seq_bits[:-1]:
        (packed,) = call(functools.partial(merge_kernel, features), [(packed_shape, F32)], [VMEM, VMEM])(
            packed, swap(packed, "seq", bit)
        )
    half_shape = ((half, width), F32)
    keep, give = call(
        functools.partial(project_kernel, steps, requests, features), [half_shape, half_shape], [VMEM, VMEM, VMEM]
    )(packed, swap(packed, "seq", seq_bits[-1]), w_out)

    tp_swaps = [("tp", bit) for bit in bits_of("tp")]
    mine, other = reduce_halves(keep, give, tp_swaps)

    n_chunks = len(chunks_of(hidden_local, 256))
    mid, keep, give = call(
        expert_kernel,
        [((tokens, width), F32), half_shape, half_shape],
        [VMEM] * 6 + [ANY, ANY],
        [
            pltpu.VMEM(w_gate_up.shape, BF16),
            pltpu.VMEM(w_down.shape, BF16),
            dma((2, n_chunks)),
            dma((n_chunks,)),
        ],
    )(mine, other, flat_in, moe_gain[None], router.T, expert_choice.reshape(tokens, -1), w_gate_up, w_down)

    mine, other = reduce_halves(keep, give, tp_swaps + [("seq", bit) for bit in seq_bits])
    low = lax.axis_index("tp") % 2 == 0
    mixture = jnp.concatenate([jnp.where(low, mine, other), jnp.where(low, other, mine)])
    return (mid + mixture).astype(BF16).reshape(steps, requests, width)


def solution(mesh):
    return jax.shard_map(
        on_device,
        mesh=mesh,
        in_specs=(
            P(),
            P(None, "seq", "tp"),
            P(None, "seq", "tp"),
            P(),
            P(),
            P(None, "tp"),
            P(),
            P(),
            P(None, None, "tp"),
            P("tp", None),
            P(),
            P(),
            P(None, ("seq", "tp"), None),
            P(("seq", "tp"), None),
        ),
        out_specs=P(),
        check_vma=False,
    )
```

```python
import functools

import jax
import jax.numpy as jnp
from jax import lax
from jax.experimental import pallas as pl
from jax.experimental.pallas import tpu as pltpu
from jax.sharding import PartitionSpec as P

HEAD_DIM = 64
FF = 2816
LANES = 128
NEG = -1e30
EPS = 1e-06
F32 = jnp.float32
BF16 = jnp.bfloat16
VMEM = pl.BlockSpec(memory_space=pltpu.VMEM)
HBM = pl.BlockSpec(memory_space=pltpu.HBM)
NT = (((1,), (1,)), ((), ()))


def dot(one, two):
    return jnp.dot(one, two, preferred_element_type=F32)


def dot_nt(one, two):
    return lax.dot_general(one, two, NT, preferred_element_type=F32)


def iota(shape, dim):
    return lax.broadcasted_iota(jnp.int32, shape, dim)


def rms_scale(values, gain_vec):
    return values * lax.rsqrt(jnp.mean(values * values, axis=-1, keepdims=True) + EPS) * gain_vec


def shift_of(size):
    assert size & (size - 1) == 0
    return size.bit_length() - 1


def over(value, size):
    return lax.shift_right_logical(value, jnp.int32(shift_of(size)))


def modulo(value, size):
    assert size & (size - 1) == 0
    return value & (size - 1)


def attend_kernel(
    steps, requests, heads, len_hbm, tokens_hbm, gain_hbm, table_hbm, rel_hbm, w_hbm, k_hbm, v_hbm,
    out_ref, len_ref, tokens_ref, gain_ref, table_ref, rel_ref, w_buf, k_buf, v_buf,
    bias_buf, score_buf, weight_buf, start_buf, step_buf, small_sem, w_sem, k_sem, v_sem,
):
    tokens = steps * requests
    group = steps * heads
    rows = requests * group
    buckets = rel_ref.shape[1]
    cache_rows, features = k_buf.shape[1:]
    small = (
        (len_hbm, len_ref),
        (table_hbm, table_ref.at[0]),
        (rel_hbm, rel_ref),
        (tokens_hbm, tokens_ref),
        (gain_hbm, gain_ref.at[0]),
    )
    small_copies = [pltpu.make_async_copy(src, dst, small_sem.at[i]) for i, (src, dst) in enumerate(small)]
    w_copies = [pltpu.make_async_copy(w_hbm.at[k], w_buf.at[k], w_sem.at[k]) for k in range(3)]
    k_copies = [pltpu.make_async_copy(k_hbm.at[r], k_buf.at[r], k_sem.at[r]) for r in range(requests)]
    v_copies = [pltpu.make_async_copy(v_hbm.at[r], v_buf.at[r], v_sem.at[r]) for r in range(requests)]
    for copy in small_copies + w_copies + k_copies + v_copies:
        copy.start()

    seq = lax.axis_index("seq")
    base = seq * cache_rows

    for copy in small_copies[:3]:
        copy.wait()
    table = table_ref[...]
    below = jnp.where(table < iota((buckets, table.shape[1]), 0), 1.0, 0.0)
    starts = jnp.sum(below, axis=1, keepdims=True).astype(jnp.int32)
    start_buf[...] = jnp.broadcast_to(starts, (buckets, LANES))

    group_head = over(iota((group, 1), 0), steps)
    level = jnp.zeros((group, buckets), F32)
    for h in range(heads):
        level = jnp.where(group_head == h, rel_ref[h : h + 1, :], level)
    for b in range(buckets):
        step_buf[b] = jnp.broadcast_to(level[:, b : b + 1], (group, LANES))

    def bias_of(pieces):
        width = pieces[0].shape[1]
        biases = [step_buf[0][:, :width]] * len(pieces)
        for b in range(1, buckets):
            start, value = start_buf[b : b + 1, :width], step_buf[b][:, :width]
            biases = [jnp.where(piece >= start, value, bias) for piece, bias in zip(pieces, biases)]
        return biases

    group_step = modulo(iota((group, 1), 0), steps)
    col_slices = [slice(c, c + LANES) for c in range(0, cache_rows, LANES)]
    offsets = [group_step - iota((1, LANES), 1) - (base + c.start) for c in col_slices]
    per_trip = 2

    def fill_bias(trip, carry):
        places, distances = [], []
        for i in range(per_trip):
            r = trip * per_trip + i
            length = len_ref[r]
            for cols, offset in zip(col_slices, offsets):
                places.append((pl.ds(pl.multiple_of(r * group, group), group), cols))
                distances.append(offset + length)
        for place, distance, bias in zip(places, distances, bias_of(distances)):
            bias_buf[place] = jnp.where(distance > group_step, bias, NEG)
        return carry

    lax.fori_loop(0, requests // per_trip, fill_bias, 0)

    for copy in small_copies[3:]:
        copy.wait()
    x = tokens_ref[...].astype(F32)
    normed = rms_scale(x, gain_ref[...]).astype(BF16)
    projected = []
    for k in range(3):
        w_copies[k].wait()
        projected.append(dot(normed, w_buf[k]).astype(BF16))
    queries, fresh_keys, fresh_values = projected

    row = iota((rows, 1), 0)
    row_step, row_head, row_request = modulo(row, steps), modulo(over(row, steps), heads), over(row, group)
    column = iota((1, tokens), 1)
    pick = jnp.where(row_step * requests + row_request == column, 1.0, 0.0).astype(BF16)
    own_head = row_head == over(iota((1, features), 1), HEAD_DIM)
    spread = jnp.where(own_head, dot(pick, queries), 0.0).astype(BF16)

    key_step, key_request = over(column, requests), modulo(column, requests)
    newest = jnp.where(seq == 0, row_step, -1)
    fresh_live = jnp.logical_and(key_step <= newest, key_request == row_request)
    (fresh_bias,) = bias_of([group_step - key_step])
    fresh_bias = jnp.concatenate([fresh_bias] * requests, axis=0)
    fresh_scores = jnp.where(fresh_live, dot_nt(spread, fresh_keys) + fresh_bias, NEG)

    for r in range(requests):
        at = slice(r * group, (r + 1) * group)
        k_copies[r].wait()
        score_buf[at, :] = dot_nt(spread[at], k_buf[r])
    scores = score_buf[...] + bias_buf[...]
    top = jnp.maximum(jnp.max(scores, axis=1, keepdims=True), jnp.max(fresh_scores, axis=1, keepdims=True))
    weights = jnp.where(scores > 0.5 * NEG, jnp.exp(scores - top), 0.0)
    fresh_weights = jnp.where(fresh_live, jnp.exp(fresh_scores - top), 0.0)
    total = jnp.sum(weights, axis=1, keepdims=True) + jnp.sum(fresh_weights, axis=1, keepdims=True)
    weight_buf[...] = weights.astype(BF16)
    score_buf[...] = dot(fresh_weights.astype(BF16), fresh_values)
    for r in range(requests):
        at = slice(r * group, (r + 1) * group)
        v_copies[r].wait()
        score_buf[at, :] += dot(weight_buf[at, :], v_buf[r])

    sums = jnp.where(own_head, score_buf[...], 0.0)
    lane = iota((1, LANES), 1)
    stats = jnp.where(lane == row_head, top, jnp.where(lane == heads + row_head, total, 0.0))
    first = iota((8, 1), 0) < steps
    for values, cols in ((sums, slice(0, features)), (stats, slice(features, features + LANES))):
        for pair in range(requests // 2):
            folded = []
            for r in (2 * pair, 2 * pair + 1):
                part = values[r * group : r * group + 8] + values[r * group + 8 : r * group + 16]
                folded.append(part + pltpu.roll(part, steps, 0))
            out_ref[8 * pair : 8 * pair + 8, cols] = jnp.where(first, folded[0], folded[1])


def widen(stats, first, features):
    heads = features // HEAD_DIM
    lane_head = over(iota((1, features), 1), HEAD_DIM)
    wide = jnp.broadcast_to(stats[:, first : first + 1], (stats.shape[0], features))
    for h in range(1, heads):
        wide = jnp.where(lane_head == h, stats[:, first + h : first + h + 1], wide)
    return wide


def merged(features, one_ref, two_ref):
    heads = features // HEAD_DIM
    one, two = one_ref[:, features:], two_ref[:, features:]
    top = jnp.maximum(one, two)
    scale_one, scale_two = jnp.exp(one - top), jnp.exp(two - top)
    totals = one * pltpu.roll(scale_one, heads, 1) + two * pltpu.roll(scale_two, heads, 1)
    sums = one_ref[:, :features] * widen(scale_one, 0, features) + two_ref[:, :features] * widen(scale_two, 0, features)
    return sums, jnp.where(iota(top.shape, 1) < heads, top, totals)


def merge_kernel(features, one_ref, two_ref, out_ref):
    sums, stats = merged(features, one_ref, two_ref)
    out_ref[:, :features] = sums
    out_ref[:, features:] = stats


def store_halves(value, bit, keep_ref, give_ref):
    half = value.shape[0] // 2
    low = lax.axis_index("tp") // bit % 2 == 0
    keep_ref[...] = jnp.where(low, value[:half], value[half:])
    give_ref[...] = jnp.where(low, value[half:], value[:half])


def project_kernel(steps, requests, features, one_ref, two_ref, w_ref, keep_ref, give_ref):
    sums, stats = merged(features, one_ref, two_ref)
    attended = (sums / widen(stats, features // HEAD_DIM, features)).astype(BF16)
    tokens = steps * requests
    row = iota((tokens, 1), 0)
    source = modulo(row, requests) * steps + over(row, requests)
    order = jnp.where(source == iota((1, tokens), 1), 1.0, 0.0).astype(BF16)
    attended = dot(order, attended).astype(BF16)
    store_halves(dot(attended, w_ref[...]), 1, keep_ref, give_ref)


def chunks_of(total, size):
    return [(at, min(size, total - at)) for at in range(0, total, size)]


def expert_kernel(
    half_ref, back_ref, tokens_ref, gain_ref, router_ref, choice_ref, up_ref, down_ref, mid_ref, keep_ref, give_ref
):
    hidden_local = down_ref.shape[0]
    half = half_ref.shape[0]
    steps, _, requests = choice_ref.shape
    low = lax.axis_index("tp") % 2 == 0
    mine, other = half_ref[...], back_ref[...]
    mid_ref[:half] = tokens_ref[:half].astype(F32) + jnp.where(low, mine, other)
    mid_ref[half:] = tokens_ref[half:].astype(F32) + jnp.where(low, other, mine)
    moe_in = rms_scale(mid_ref[...], gain_ref[...]).astype(BF16)
    logits = dot_nt(moe_in, router_ref[...])
    expert = iota((1, logits.shape[1]), 1)
    own = iota((requests, 1), 0) == iota((1, requests), 1)
    choices, chosen = [], []
    for pick in range(2):
        column = [
            jnp.sum(jnp.where(own, choice_ref[t, pick : pick + 1, :].astype(F32), 0.0), axis=1, keepdims=True)
            for t in range(steps)
        ]
        choices.append(jnp.concatenate(column, axis=0).astype(jnp.int32))
        chosen.append(jnp.sum(jnp.where(expert == choices[pick], logits, 0.0), axis=1, keepdims=True))
    first = 1.0 / (1.0 + jnp.exp(chosen[1] - chosen[0]))
    second = 1.0 - first
    device = lax.axis_index("seq") * lax.axis_size("tp") + lax.axis_index("tp")
    total = jnp.zeros(mid_ref.shape, F32)
    for at, size in chunks_of(hidden_local, 256):
        column_expert = (device * hidden_local + at + iota((1, size), 1)) // FF
        coef = jnp.where(column_expert == choices[0], first, jnp.where(column_expert == choices[1], second, 0.0))
        gate = dot_nt(moe_in, up_ref[0, at : at + size, :])
        up = dot_nt(moe_in, up_ref[1, at : at + size, :])
        hidden = (jax.nn.gelu(gate, approximate=True) * up * coef).astype(BF16)
        total = total + dot(hidden, down_ref[at : at + size, :])
    store_halves(total, 1, keep_ref, give_ref)


def swap(value, axis, bit):
    return lax.ppermute(value, axis, [(i, i ^ bit) for i in range(lax.axis_size(axis))])


def bits_of(axis):
    size = lax.axis_size(axis)
    assert size & (size - 1) == 0
    return [1 << k for k in range(size.bit_length() - 1)]


def reduce_halves(keep, give, swaps):
    half = keep + swap(give, *swaps[0])
    for axis, bit in swaps[1:]:
        half = half + swap(half, axis, bit)
    return half, swap(half, *swaps[0])


def in_hbm(value):
    return pltpu.with_memory_space_constraint(value, pltpu.HBM)


def call(kernel, out_shape, in_specs, limit, scratch=()):
    shapes = [jax.ShapeDtypeStruct(shape, dtype) for shape, dtype in out_shape]
    return pl.pallas_call(
        kernel,
        out_shape=shapes,
        in_specs=in_specs,
        out_specs=[VMEM] * len(shapes),
        scratch_shapes=list(scratch),
        compiler_params=pltpu.CompilerParams(vmem_limit_bytes=limit << 20),
    )


def on_device(
    tokens_in,
    key_cache,
    value_cache,
    cache_len,
    bucket_table,
    rel_bias,
    attn_gain,
    moe_gain,
    w_qkv,
    w_out,
    router,
    expert_choice,
    w_gate_up,
    w_down,
):
    steps, requests, width = tokens_in.shape
    tokens = steps * requests
    half = tokens // 2
    _, cache_rows, features = key_cache.shape
    heads = features // HEAD_DIM
    rows = tokens * heads
    buckets = rel_bias.shape[0]
    hidden_local = w_down.shape[0]
    packed_shape = (tokens, features + LANES)
    flat_in = tokens_in.reshape(tokens, width)
    dma = pltpu.SemaphoreType.DMA

    (packed,) = call(
        functools.partial(attend_kernel, steps, requests, heads),
        [(packed_shape, F32)],
        [HBM] * 8,
        16,
        [
            pltpu.SMEM(cache_len.shape, jnp.int32),
            pltpu.VMEM(flat_in.shape, BF16),
            pltpu.VMEM((1, width), F32),
            pltpu.VMEM((1,) + bucket_table.shape, jnp.int32),
            pltpu.VMEM((heads, buckets), F32),
            pltpu.VMEM(w_qkv.shape, BF16),
            pltpu.VMEM(key_cache.shape, BF16),
            pltpu.VMEM(value_cache.shape, BF16),
            pltpu.VMEM((rows, cache_rows), F32),
            pltpu.VMEM((rows, cache_rows), F32),
            pltpu.VMEM((rows, cache_rows), BF16),
            pltpu.VMEM((buckets, LANES), jnp.int32),
            pltpu.VMEM((buckets, steps * heads, LANES), F32),
            dma((5,)),
            dma((3,)),
            dma((requests,)),
            dma((requests,)),
        ],
    )(*map(in_hbm, (cache_len, flat_in, attn_gain, bucket_table, rel_bias.T, w_qkv, key_cache, value_cache)))

    seq_bits = bits_of("seq")
    for bit in seq_bits[:-1]:
        (packed,) = call(functools.partial(merge_kernel, features), [(packed_shape, F32)], [VMEM, VMEM], 2)(
            packed, swap(packed, "seq", bit)
        )
    half_shape = ((half, width), F32)
    keep, give = call(
        functools.partial(project_kernel, steps, requests, features), [half_shape, half_shape], [VMEM] * 3, 4
    )(packed, swap(packed, "seq", seq_bits[-1]), w_out)

    tp_swaps = [("tp", bit) for bit in bits_of("tp")]
    mine, other = reduce_halves(keep, give, tp_swaps)

    mid, keep, give = call(expert_kernel, [((tokens, width), F32), half_shape, half_shape], [VMEM] * 8, 8)(
        mine, other, flat_in, moe_gain[None], router.T, expert_choice.transpose(0, 2, 1), w_gate_up, w_down
    )

    mine, other = reduce_halves(keep, give, tp_swaps + [("seq", bit) for bit in seq_bits])
    low = lax.axis_index("tp") % 2 == 0
    mixture = jnp.concatenate([jnp.where(low, mine, other), jnp.where(low, other, mine)])
    return (mid + mixture).astype(BF16).reshape(steps, requests, width)


def solution(mesh):
    return jax.shard_map(
        on_device,
        mesh=mesh,
        in_specs=(
            P(),
            P(None, "seq", "tp"),
            P(None, "seq", "tp"),
            P(),
            P(),
            P(None, "tp"),
            P(),
            P(),
            P(None, None, "tp"),
            P("tp", None),
            P(),
            P(),
            P(None, ("seq", "tp"), None),
            P(("seq", "tp"), None),
        ),
        out_specs=P(),
        check_vma=False,
    )
```

```python
import functools

import jax
import jax.numpy as jnp
from jax import lax
from jax.experimental import pallas as pl
from jax.experimental.pallas import tpu as pltpu
from jax.sharding import PartitionSpec as P

HEAD_DIM = 64
FF = 2816
LANES = 128
NEG = -1e30
EPS = 1e-06
F32 = jnp.float32
BF16 = jnp.bfloat16
VMEM = pl.BlockSpec(memory_space=pltpu.VMEM)
HBM = pl.BlockSpec(memory_space=pltpu.HBM)
NT = (((1,), (1,)), ((), ()))


def dot(one, two):
    return jnp.dot(one, two, preferred_element_type=F32)


def dot_nt(one, two):
    return lax.dot_general(one, two, NT, preferred_element_type=F32)


def iota(shape, dim):
    return lax.broadcasted_iota(jnp.int32, shape, dim)


def rms_scale(values, gain_vec):
    return values * lax.rsqrt(jnp.mean(values * values, axis=-1, keepdims=True) + EPS) * gain_vec


def shift_of(size):
    assert size & (size - 1) == 0
    return size.bit_length() - 1


def over(value, size):
    return lax.shift_right_logical(value, jnp.int32(shift_of(size)))


def modulo(value, size):
    assert size & (size - 1) == 0
    return value & (size - 1)


def attend_kernel(
    steps, requests, heads, len_hbm, tokens_hbm, gain_hbm, table_hbm, rel_hbm, w_hbm, k_hbm, v_hbm,
    out_ref, len_ref, tokens_ref, gain_ref, table_ref, rel_ref, w_buf, k_buf, v_buf,
    bias_buf, score_buf, weight_buf, start_buf, step_buf, small_sem, w_sem, k_sem, v_sem,
):
    tokens = steps * requests
    group = steps * heads
    rows = requests * group
    buckets = rel_ref.shape[1]
    cache_rows, features = k_buf.shape[1:]
    small = (
        (len_hbm, len_ref),
        (table_hbm, table_ref.at[0]),
        (rel_hbm, rel_ref),
        (tokens_hbm, tokens_ref),
        (gain_hbm, gain_ref.at[0]),
    )
    small_copies = [pltpu.make_async_copy(src, dst, small_sem.at[i]) for i, (src, dst) in enumerate(small)]
    w_copies = [pltpu.make_async_copy(w_hbm.at[k], w_buf.at[k], w_sem.at[k]) for k in range(3)]
    k_copies = [pltpu.make_async_copy(k_hbm.at[r], k_buf.at[r], k_sem.at[r]) for r in range(requests)]
    v_copies = [pltpu.make_async_copy(v_hbm.at[r], v_buf.at[r], v_sem.at[r]) for r in range(requests)]
    for copy in small_copies + w_copies + k_copies + v_copies:
        copy.start()

    seq = lax.axis_index("seq")
    base = seq * cache_rows

    for copy in small_copies[:3]:
        copy.wait()
    table = table_ref[...]
    below = jnp.where(table < iota((buckets, table.shape[1]), 0), 1.0, 0.0)
    starts = jnp.sum(below, axis=1, keepdims=True).astype(jnp.int32)
    start_buf[...] = jnp.broadcast_to(starts, (buckets, LANES))

    group_head = over(iota((group, 1), 0), steps)
    level = jnp.zeros((group, buckets), F32)
    for h in range(heads):
        level = jnp.where(group_head == h, rel_ref[h : h + 1, :], level)
    for b in range(buckets):
        step_buf[b] = jnp.broadcast_to(level[:, b : b + 1], (group, LANES))

    def bias_of(pieces):
        width = pieces[0].shape[1]
        biases = [step_buf[0][:, :width]] * len(pieces)
        for b in range(1, buckets):
            start, value = start_buf[b : b + 1, :width], step_buf[b][:, :width]
            biases = [jnp.where(piece >= start, value, bias) for piece, bias in zip(pieces, biases)]
        return biases

    group_step = modulo(iota((group, 1), 0), steps)
    col_slices = [slice(c, c + LANES) for c in range(0, cache_rows, LANES)]
    offsets = [group_step - iota((1, LANES), 1) - (base + c.start) for c in col_slices]
    per_trip = 2

    def fill_bias(trip, carry):
        places, distances = [], []
        for i in range(per_trip):
            r = trip * per_trip + i
            length = len_ref[r]
            for cols, offset in zip(col_slices, offsets):
                places.append((pl.ds(pl.multiple_of(r * group, group), group), cols))
                distances.append(offset + length)
        for place, distance, bias in zip(places, distances, bias_of(distances)):
            bias_buf[place] = jnp.where(distance > group_step, bias, NEG)
        return carry

    lax.fori_loop(0, requests // per_trip, fill_bias, 0)

    for copy in small_copies[3:]:
        copy.wait()
    x = tokens_ref[...].astype(F32)
    normed = rms_scale(x, gain_ref[...]).astype(BF16)
    projected = []
    for k in range(3):
        w_copies[k].wait()
        projected.append(dot(normed, w_buf[k]).astype(BF16))
    queries, fresh_keys, fresh_values = projected

    row = iota((rows, 1), 0)
    row_step, row_head, row_request = modulo(row, steps), modulo(over(row, steps), heads), over(row, group)
    column = iota((1, tokens), 1)
    pick = jnp.where(row_step * requests + row_request == column, 1.0, 0.0).astype(BF16)
    own_head = row_head == over(iota((1, features), 1), HEAD_DIM)
    spread = jnp.where(own_head, dot(pick, queries), 0.0).astype(BF16)

    key_step, key_request = over(column, requests), modulo(column, requests)
    newest = jnp.where(seq == 0, row_step, -1)
    fresh_live = jnp.logical_and(key_step <= newest, key_request == row_request)
    (fresh_bias,) = bias_of([group_step - key_step])
    fresh_bias = jnp.concatenate([fresh_bias] * requests, axis=0)
    fresh_scores = jnp.where(fresh_live, dot_nt(spread, fresh_keys) + fresh_bias, NEG)

    for copy in k_copies:
        copy.wait()
    for r in range(requests):
        at = slice(r * group, (r + 1) * group)
        score_buf[at, :] = dot_nt(spread[at], k_buf[r])
    scores = score_buf[...] + bias_buf[...]
    top = jnp.maximum(jnp.max(scores, axis=1, keepdims=True), jnp.max(fresh_scores, axis=1, keepdims=True))
    weights = jnp.where(scores > 0.5 * NEG, jnp.exp(scores - top), 0.0)
    fresh_weights = jnp.where(fresh_live, jnp.exp(fresh_scores - top), 0.0)
    total = jnp.sum(weights, axis=1, keepdims=True) + jnp.sum(fresh_weights, axis=1, keepdims=True)
    weight_buf[...] = weights.astype(BF16)
    score_buf[...] = dot(fresh_weights.astype(BF16), fresh_values)
    for copy in v_copies:
        copy.wait()
    for r in range(requests):
        at = slice(r * group, (r + 1) * group)
        score_buf[at, :] += dot(weight_buf[at, :], v_buf[r])

    sums = jnp.where(own_head, score_buf[...], 0.0)
    lane = iota((1, LANES), 1)
    stats = jnp.where(lane == row_head, top, jnp.where(lane == heads + row_head, total, 0.0))
    first = iota((8, 1), 0) < steps

    def fold(values):
        pairs = []
        for pair in range(requests // 2):
            folded = []
            for r in (2 * pair, 2 * pair + 1):
                part = values[r * group : r * group + 8] + values[r * group + 8 : r * group + 16]
                folded.append(part + pltpu.roll(part, steps, 0))
            pairs.append(jnp.where(first, folded[0], folded[1]))
        return jnp.concatenate(pairs, axis=0)

    out_ref[:tokens, :] = fold(sums)
    out_ref[tokens:, :] = jnp.zeros((2 * heads, features), F32)
    out_ref[tokens:, :LANES] = turned(fold(stats))[: 2 * heads]


def turned(value):
    rows = value.shape[0]
    if rows < LANES:
        value = jnp.concatenate([value, jnp.zeros((LANES - rows, LANES), F32)], axis=0)
    return value.T


def widen(columns, first, heads):
    lane_head = over(iota((1, heads * HEAD_DIM), 1), HEAD_DIM)
    wide = jnp.broadcast_to(columns[:, first : first + 1], (columns.shape[0], heads * HEAD_DIM))
    for h in range(1, heads):
        wide = jnp.where(lane_head == h, columns[:, first + h : first + h + 1], wide)
    return wide


def tree(operation, values):
    while len(values) > 1:
        values = [operation(*values[i : i + 2]) for i in range(0, len(values), 2)]
    return values[0]


def merge_parts(tokens, parts):
    heads = parts[0].shape[1] // HEAD_DIM
    stats = [part[tokens:, :LANES] for part in parts]
    top = tree(jnp.maximum, stats)
    scales = [jnp.exp(stat - top) for stat in stats]
    totals = tree(jnp.add, [stat * pltpu.roll(scale, heads, 0) for stat, scale in zip(stats, scales)])
    stat = jnp.where(iota((2 * heads, 1), 0) < heads, top, totals)
    columns = turned(jnp.concatenate(scales + [stat], axis=0))[:tokens]
    sums = tree(
        jnp.add, [part[:tokens, :] * widen(columns, 2 * heads * i, heads) for i, part in enumerate(parts)]
    )
    return sums, stat, widen(columns, 2 * heads * len(parts) + heads, heads)


def merge_kernel(tokens, *refs):
    out_ref = refs[-1]
    sums, stat, _ = merge_parts(tokens, refs[:-1])
    out_ref[:tokens, :] = sums
    out_ref[tokens:, :] = jnp.zeros((stat.shape[0], sums.shape[1]), F32)
    out_ref[tokens:, :LANES] = stat


def store_halves(value, bit, keep_ref, give_ref):
    half = value.shape[0] // 2
    low = lax.axis_index("tp") // bit % 2 == 0
    keep_ref[...] = jnp.where(low, value[:half], value[half:])
    give_ref[...] = jnp.where(low, value[half:], value[:half])


def project_kernel(steps, requests, one_ref, two_ref, w_ref, keep_ref, give_ref):
    tokens = steps * requests
    sums, _, totals = merge_parts(tokens, (one_ref, two_ref))
    attended = (sums / totals).astype(BF16)
    row = iota((tokens, 1), 0)
    source = modulo(row, requests) * steps + over(row, requests)
    order = jnp.where(source == iota((1, tokens), 1), 1.0, 0.0).astype(BF16)
    attended = dot(order, attended).astype(BF16)
    store_halves(dot(attended, w_ref[...]), 1, keep_ref, give_ref)


def chunks_of(total, size):
    return [(at, min(size, total - at)) for at in range(0, total, size)]


def expert_kernel(
    half_ref, back_ref, tokens_ref, gain_ref, router_ref, choice_ref, up_ref, down_hbm,
    mid_ref, keep_ref, give_ref, down_ref, down_sem,
):
    hidden_local = down_ref.shape[0]
    chunks = chunks_of(hidden_local, 256)
    copies = []
    for i, (at, size) in enumerate(chunks):
        copies.append(pltpu.make_async_copy(down_hbm.at[pl.ds(at, size)], down_ref.at[pl.ds(at, size)], down_sem.at[i]))
        copies[-1].start()
    half = half_ref.shape[0]
    steps, _, requests = choice_ref.shape
    low = lax.axis_index("tp") % 2 == 0
    mine, other = half_ref[...], back_ref[...]
    mid_ref[:half] = tokens_ref[:half].astype(F32) + jnp.where(low, mine, other)
    mid_ref[half:] = tokens_ref[half:].astype(F32) + jnp.where(low, other, mine)
    moe_in = rms_scale(mid_ref[...], gain_ref[...]).astype(BF16)
    logits = dot_nt(moe_in, router_ref[...])
    expert = iota((1, logits.shape[1]), 1)
    own = iota((requests, 1), 0) == iota((1, requests), 1)
    choices, chosen = [], []
    for pick in range(2):
        column = [
            jnp.sum(jnp.where(own, choice_ref[t, pick : pick + 1, :].astype(F32), 0.0), axis=1, keepdims=True)
            for t in range(steps)
        ]
        choices.append(jnp.concatenate(column, axis=0).astype(jnp.int32))
        chosen.append(jnp.sum(jnp.where(expert == choices[pick], logits, 0.0), axis=1, keepdims=True))
    first = 1.0 / (1.0 + jnp.exp(chosen[1] - chosen[0]))
    second = 1.0 - first
    device = lax.axis_index("seq") * lax.axis_size("tp") + lax.axis_index("tp")
    total = jnp.zeros(mid_ref.shape, F32)
    hiddens = []
    for at, size in chunks:
        column_expert = (device * hidden_local + at + iota((1, size), 1)) // FF
        coef = jnp.where(column_expert == choices[0], first, jnp.where(column_expert == choices[1], second, 0.0))
        gate = dot_nt(moe_in, up_ref[0, at : at + size, :])
        up = dot_nt(moe_in, up_ref[1, at : at + size, :])
        hiddens.append((jax.nn.gelu(gate, approximate=True) * up * coef).astype(BF16))
    for copy in copies:
        copy.wait()
    for (at, size), hidden in zip(chunks, hiddens):
        total = total + dot(hidden, down_ref[at : at + size, :])
    store_halves(total, 1, keep_ref, give_ref)


def device_bits(axis):
    size = lax.axis_size(axis)
    assert size & (size - 1) == 0
    return [(axis, 1 << k) for k in range(size.bit_length() - 1)]


def swap(value, *bits):
    sizes = {axis: lax.axis_size(axis) for axis in ("seq", "tp") if axis in dict(bits)}
    flips = {axis: sum(bit for other, bit in bits if other == axis) for axis in sizes}
    if len(sizes) == 1:
        (axis,) = sizes
        return lax.ppermute(value, axis, [(i, i ^ flips[axis]) for i in range(sizes[axis])])
    (one, two) = sizes
    flat = [i * sizes[two] + j for i in range(sizes[one]) for j in range(sizes[two])]
    there = [(i ^ flips[one]) * sizes[two] + (j ^ flips[two]) for i in range(sizes[one]) for j in range(sizes[two])]
    return lax.ppermute(value, (one, two), list(zip(flat, there)))


def gathered(value, bits):
    parts = [value]
    for bit in bits:
        parts.append(swap(value, bit))
    if len(bits) == 2:
        parts.append(swap(value, *bits))
    return parts


def stages(bits):
    return [bits[:2]] + [[bit] for bit in bits[2:]] if len(bits) > 2 else [[bit] for bit in bits]


def reduce_halves(keep, give, split, groups):
    half = keep + swap(give, split)
    for bits in groups:
        half = tree(jnp.add, gathered(half, bits))
    return half, swap(half, split)


def in_hbm(value):
    return pltpu.with_memory_space_constraint(value, pltpu.HBM)


def call(kernel, out_shape, in_specs, limit, scratch=()):
    shapes = [jax.ShapeDtypeStruct(shape, dtype) for shape, dtype in out_shape]
    return pl.pallas_call(
        kernel,
        out_shape=shapes,
        in_specs=in_specs,
        out_specs=[VMEM] * len(shapes),
        scratch_shapes=list(scratch),
        compiler_params=pltpu.CompilerParams(vmem_limit_bytes=limit << 20),
    )


def on_device(
    tokens_in,
    key_cache,
    value_cache,
    cache_len,
    bucket_table,
    rel_bias,
    attn_gain,
    moe_gain,
    w_qkv,
    w_out,
    router,
    expert_choice,
    w_gate_up,
    w_down,
):
    steps, requests, width = tokens_in.shape
    tokens = steps * requests
    half = tokens // 2
    _, cache_rows, features = key_cache.shape
    heads = features // HEAD_DIM
    rows = tokens * heads
    buckets = rel_bias.shape[0]
    hidden_local = w_down.shape[0]
    packed_shape = (tokens + 2 * heads, features)
    flat_in = tokens_in.reshape(tokens, width)
    dma = pltpu.SemaphoreType.DMA

    (packed,) = call(
        functools.partial(attend_kernel, steps, requests, heads),
        [(packed_shape, F32)],
        [HBM] * 8,
        16,
        [
            pltpu.SMEM(cache_len.shape, jnp.int32),
            pltpu.VMEM(flat_in.shape, BF16),
            pltpu.VMEM((1, width), F32),
            pltpu.VMEM((1,) + bucket_table.shape, jnp.int32),
            pltpu.VMEM((heads, buckets), F32),
            pltpu.VMEM(w_qkv.shape, BF16),
            pltpu.VMEM(key_cache.shape, BF16),
            pltpu.VMEM(value_cache.shape, BF16),
            pltpu.VMEM((rows, cache_rows), F32),
            pltpu.VMEM((rows, cache_rows), F32),
            pltpu.VMEM((rows, cache_rows), BF16),
            pltpu.VMEM((buckets, LANES), jnp.int32),
            pltpu.VMEM((buckets, steps * heads, LANES), F32),
            dma((5,)),
            dma((3,)),
            dma((requests,)),
            dma((requests,)),
        ],
    )(*map(in_hbm, (cache_len, flat_in, attn_gain, bucket_table, rel_bias.T, w_qkv, key_cache, value_cache)))

    packed, w_gate_up = lax.optimization_barrier((packed, w_gate_up))
    seq_bits, tp_bits = device_bits("seq"), device_bits("tp")
    seq_stages = stages(seq_bits)
    for bits in seq_stages[:-1]:
        parts = gathered(packed, bits)
        (packed,) = call(functools.partial(merge_kernel, tokens), [(packed_shape, F32)], [VMEM] * len(parts), 2)(*parts)
    half_shape = ((half, width), F32)
    keep, give = call(
        functools.partial(project_kernel, steps, requests), [half_shape, half_shape], [VMEM] * 3, 4
    )(packed, swap(packed, *seq_stages[-1]), w_out)

    mine, other = reduce_halves(keep, give, tp_bits[0], [[bit] for bit in tp_bits[1:]])

    n_chunks = len(chunks_of(hidden_local, 256))
    mid, keep, give = call(
        expert_kernel,
        [((tokens, width), F32), half_shape, half_shape],
        [VMEM] * 7 + [HBM],
        12,
        [pltpu.VMEM(w_down.shape, BF16), dma((n_chunks,))],
    )(
        mine, other, flat_in, moe_gain[None], router.T, expert_choice.transpose(0, 2, 1), w_gate_up, in_hbm(w_down)
    )

    mine, other = reduce_halves(keep, give, tp_bits[0], stages(tp_bits[1:] + seq_bits))
    low = lax.axis_index("tp") % 2 == 0
    mixture = jnp.concatenate([jnp.where(low, mine, other), jnp.where(low, other, mine)])
    return (mid + mixture).astype(BF16).reshape(steps, requests, width)


def solution(mesh):
    return jax.shard_map(
        on_device,
        mesh=mesh,
        in_specs=(
            P(),
            P(None, "seq", "tp"),
            P(None, "seq", "tp"),
            P(),
            P(),
            P(None, "tp"),
            P(),
            P(),
            P(None, None, "tp"),
            P("tp", None),
            P(),
            P(),
            P(None, ("seq", "tp"), None),
            P(("seq", "tp"), None),
        ),
        out_specs=P(),
        check_vma=False,
    )
```

```python
import functools

import jax
import jax.numpy as jnp
from jax import lax
from jax.experimental import pallas as pl
from jax.experimental.pallas import tpu as pltpu
from jax.sharding import PartitionSpec as P

HEAD_DIM = 64
FF = 2816
LANES = 128
NEG = -1e30
EPS = 1e-06
F32 = jnp.float32
BF16 = jnp.bfloat16
VMEM = pl.BlockSpec(memory_space=pltpu.VMEM)
HBM = pl.BlockSpec(memory_space=pltpu.HBM)
NT = (((1,), (1,)), ((), ()))


def dot(one, two):
    return jnp.dot(one, two, preferred_element_type=F32)


def dot_nt(one, two):
    return lax.dot_general(one, two, NT, preferred_element_type=F32)


def iota(shape, dim):
    return lax.broadcasted_iota(jnp.int32, shape, dim)


def rms_scale(values, gain_vec):
    return values * lax.rsqrt(jnp.mean(values * values, axis=-1, keepdims=True) + EPS) * gain_vec


def shift_of(size):
    assert size & (size - 1) == 0
    return size.bit_length() - 1


def over(value, size):
    return lax.shift_right_logical(value, jnp.int32(shift_of(size)))


def modulo(value, size):
    assert size & (size - 1) == 0
    return value & (size - 1)


def attend_kernel(
    steps, requests, heads, len_hbm, tokens_hbm, gain_hbm, table_hbm, rel_hbm, w_hbm, k_hbm, v_hbm,
    out_ref, len_ref, tokens_ref, gain_ref, table_ref, rel_ref, w_buf, k_buf, v_buf,
    bias_buf, score_buf, weight_buf, start_buf, step_buf, small_sem, w_sem, k_sem, v_sem,
):
    tokens = steps * requests
    group = steps * heads
    rows = requests * group
    buckets = rel_ref.shape[1]
    cache_rows, features = k_buf.shape[1:]
    small = (
        (len_hbm, len_ref),
        (table_hbm, table_ref.at[0]),
        (rel_hbm, rel_ref),
        (tokens_hbm, tokens_ref),
        (gain_hbm, gain_ref.at[0]),
    )
    small_copies = [pltpu.make_async_copy(src, dst, small_sem.at[i]) for i, (src, dst) in enumerate(small)]
    w_copies = [pltpu.make_async_copy(w_hbm.at[k], w_buf.at[k], w_sem.at[k]) for k in range(3)]
    per_copy = requests // k_sem.shape[0]
    blocks = [pl.ds(i * per_copy, per_copy) for i in range(k_sem.shape[0])]
    k_copies = [pltpu.make_async_copy(k_hbm.at[b], k_buf.at[b], k_sem.at[i]) for i, b in enumerate(blocks)]
    v_copies = [pltpu.make_async_copy(v_hbm.at[b], v_buf.at[b], v_sem.at[i]) for i, b in enumerate(blocks)]
    for copy in small_copies + w_copies:
        copy.start()

    seq = lax.axis_index("seq")
    base = seq * cache_rows

    for copy in small_copies[:3]:
        copy.wait()
    table = table_ref[...]
    below = jnp.where(table < iota((buckets, table.shape[1]), 0), 1.0, 0.0)
    starts = jnp.sum(below, axis=1, keepdims=True).astype(jnp.int32)
    start_buf[...] = jnp.broadcast_to(starts, (buckets, LANES))

    group_head = over(iota((group, 1), 0), steps)
    level = jnp.zeros((group, buckets), F32)
    for h in range(heads):
        level = jnp.where(group_head == h, rel_ref[h : h + 1, :], level)
    for b in range(buckets):
        step_buf[b] = jnp.broadcast_to(level[:, b : b + 1], (group, LANES))

    def bias_of(pieces):
        width = pieces[0].shape[1]
        biases = [step_buf[0][:, :width]] * len(pieces)
        for b in range(1, buckets):
            start, value = start_buf[b : b + 1, :width], step_buf[b][:, :width]
            biases = [jnp.where(piece >= start, value, bias) for piece, bias in zip(pieces, biases)]
        return biases

    group_step = modulo(iota((group, 1), 0), steps)
    col_slices = [slice(c, c + LANES) for c in range(0, cache_rows, LANES)]
    offsets = [group_step - iota((1, LANES), 1) - (base + c.start) for c in col_slices]
    per_trip = 2

    def fill_bias(trip, carry):
        places, distances = [], []
        for i in range(per_trip):
            r = trip * per_trip + i
            length = len_ref[r]
            for cols, offset in zip(col_slices, offsets):
                places.append((pl.ds(pl.multiple_of(r * group, group), group), cols))
                distances.append(offset + length)
        for place, distance, bias in zip(places, distances, bias_of(distances)):
            bias_buf[place] = jnp.where(distance > group_step, bias, NEG)
        return carry

    for copy in k_copies:
        copy.start()
    lax.fori_loop(0, requests // per_trip, fill_bias, 0)
    for copy in v_copies:
        copy.start()

    for copy in small_copies[3:]:
        copy.wait()
    x = tokens_ref[...].astype(F32)
    normed = rms_scale(x, gain_ref[...]).astype(BF16)
    projected = []
    for k in range(3):
        w_copies[k].wait()
        projected.append(dot(normed, w_buf[k]).astype(BF16))
    queries, fresh_keys, fresh_values = projected

    row = iota((rows, 1), 0)
    row_step, row_head, row_request = modulo(row, steps), modulo(over(row, steps), heads), over(row, group)
    column = iota((1, tokens), 1)
    pick = jnp.where(row_step * requests + row_request == column, 1.0, 0.0).astype(BF16)
    own_head = row_head == over(iota((1, features), 1), HEAD_DIM)
    spread = jnp.where(own_head, dot(pick, queries), 0.0).astype(BF16)

    key_step, key_request = over(column, requests), modulo(column, requests)
    newest = jnp.where(seq == 0, row_step, -1)
    fresh_live = jnp.logical_and(key_step <= newest, key_request == row_request)
    (fresh_bias,) = bias_of([group_step - key_step])
    fresh_bias = jnp.concatenate([fresh_bias] * requests, axis=0)
    fresh_scores = jnp.where(fresh_live, dot_nt(spread, fresh_keys) + fresh_bias, NEG)

    for copy in k_copies:
        copy.wait()
    for r in range(requests):
        at = slice(r * group, (r + 1) * group)
        score_buf[at, :] = dot_nt(spread[at], k_buf[r])
    scores = score_buf[...] + bias_buf[...]
    top = jnp.maximum(jnp.max(scores, axis=1, keepdims=True), jnp.max(fresh_scores, axis=1, keepdims=True))
    weights = jnp.where(scores > 0.5 * NEG, jnp.exp(scores - top), 0.0)
    fresh_weights = jnp.where(fresh_live, jnp.exp(fresh_scores - top), 0.0)
    total = jnp.sum(weights, axis=1, keepdims=True) + jnp.sum(fresh_weights, axis=1, keepdims=True)
    weight_buf[...] = weights.astype(BF16)
    score_buf[...] = dot(fresh_weights.astype(BF16), fresh_values)
    for copy in v_copies:
        copy.wait()

    lane = iota((1, LANES), 1)
    stats = jnp.where(lane == row_head, top, jnp.where(lane == heads + row_head, total, 0.0))
    group_own = own_head[:group]
    first = iota((8, 1), 0) < steps

    def folded(part):
        half = part[:8] + part[8:]
        return half + pltpu.roll(half, steps, 0)

    stat_pairs = []
    for pair in range(requests // 2):
        sums, stat_parts = [], []
        for r in (2 * pair, 2 * pair + 1):
            at = slice(r * group, (r + 1) * group)
            sums.append(folded(jnp.where(group_own, dot(weight_buf[at, :], v_buf[r]) + score_buf[at, :], 0.0)))
            stat_parts.append(folded(stats[at]))
        out_ref[8 * pair : 8 * pair + 8, :] = jnp.where(first, sums[0], sums[1])
        stat_pairs.append(jnp.where(first, stat_parts[0], stat_parts[1]))
    out_ref[tokens:, :] = jnp.zeros((2 * heads, features), F32)
    out_ref[tokens:, :LANES] = turned(jnp.concatenate(stat_pairs, axis=0))[: 2 * heads]


def turned(value):
    rows = value.shape[0]
    if rows < LANES:
        value = jnp.concatenate([value, jnp.zeros((LANES - rows, LANES), F32)], axis=0)
    return value.T


def widen(columns, first, heads):
    lane_head = over(iota((1, heads * HEAD_DIM), 1), HEAD_DIM)
    wide = jnp.broadcast_to(columns[:, first : first + 1], (columns.shape[0], heads * HEAD_DIM))
    for h in range(1, heads):
        wide = jnp.where(lane_head == h, columns[:, first + h : first + h + 1], wide)
    return wide


def tree(operation, values):
    while len(values) > 1:
        values = [operation(*values[i : i + 2]) for i in range(0, len(values), 2)]
    return values[0]


def merge_parts(tokens, parts):
    heads = parts[0].shape[1] // HEAD_DIM
    stats = [part[tokens:, :LANES] for part in parts]
    top = tree(jnp.maximum, stats)
    scales = [jnp.exp(stat - top) for stat in stats]
    totals = tree(jnp.add, [stat * pltpu.roll(scale, heads, 0) for stat, scale in zip(stats, scales)])
    stat = jnp.where(iota((2 * heads, 1), 0) < heads, top, totals)
    columns = turned(jnp.concatenate(scales + [stat], axis=0))[:tokens]
    sums = tree(
        jnp.add, [part[:tokens, :] * widen(columns, 2 * heads * i, heads) for i, part in enumerate(parts)]
    )
    return sums, stat, widen(columns, 2 * heads * len(parts) + heads, heads)


def merge_kernel(tokens, *refs):
    out_ref = refs[-1]
    sums, stat, _ = merge_parts(tokens, refs[:-1])
    out_ref[:tokens, :] = sums
    out_ref[tokens:, :] = jnp.zeros((stat.shape[0], sums.shape[1]), F32)
    out_ref[tokens:, :LANES] = stat


def store_halves(value, bit, keep_ref, give_ref):
    half = value.shape[0] // 2
    low = lax.axis_index("tp") // bit % 2 == 0
    keep_ref[...] = jnp.where(low, value[:half], value[half:])
    give_ref[...] = jnp.where(low, value[half:], value[:half])


def project_kernel(steps, requests, one_ref, two_ref, w_ref, keep_ref, give_ref):
    tokens = steps * requests
    sums, _, totals = merge_parts(tokens, (one_ref, two_ref))
    attended = (sums / totals).astype(BF16)
    row = iota((tokens, 1), 0)
    source = modulo(row, requests) * steps + over(row, requests)
    order = jnp.where(source == iota((1, tokens), 1), 1.0, 0.0).astype(BF16)
    attended = dot(order, attended).astype(BF16)
    store_halves(dot(attended, w_ref[...]), 1, keep_ref, give_ref)


def chunks_of(total, size):
    return [(at, min(size, total - at)) for at in range(0, total, size)]


def expert_kernel(
    half_ref, back_ref, tokens_ref, gain_ref, router_ref, choice_ref, up_ref, down_hbm,
    mid_ref, one_ref, two_ref, three_ref, four_ref, down_ref, down_sem,
):
    sum_refs = (one_ref, two_ref, three_ref, four_ref)
    down_copy = pltpu.make_async_copy(down_hbm, down_ref, down_sem)
    down_copy.start()
    hidden_local = down_ref.shape[0]
    half = half_ref.shape[0]
    steps, _, requests = choice_ref.shape
    low = lax.axis_index("tp") % 2 == 0
    mine, other = half_ref[...], back_ref[...]
    mid_ref[:half] = tokens_ref[:half].astype(F32) + jnp.where(low, mine, other)
    mid_ref[half:] = tokens_ref[half:].astype(F32) + jnp.where(low, other, mine)
    moe_in = rms_scale(mid_ref[...], gain_ref[...]).astype(BF16)
    logits = dot_nt(moe_in, router_ref[...])
    expert = iota((1, logits.shape[1]), 1)
    own = iota((requests, 1), 0) == iota((1, requests), 1)
    choices, chosen = [], []
    for pick in range(2):
        column = [
            jnp.sum(jnp.where(own, choice_ref[t, pick : pick + 1, :].astype(F32), 0.0), axis=1, keepdims=True)
            for t in range(steps)
        ]
        choices.append(jnp.concatenate(column, axis=0).astype(jnp.int32))
        chosen.append(jnp.sum(jnp.where(expert == choices[pick], logits, 0.0), axis=1, keepdims=True))
    first = 1.0 / (1.0 + jnp.exp(chosen[1] - chosen[0]))
    second = 1.0 - first
    device = lax.axis_index("seq") * lax.axis_size("tp") + lax.axis_index("tp")
    total = jnp.zeros(mid_ref.shape, F32)
    hiddens = []
    chunks = chunks_of(hidden_local, 256)
    for at, size in chunks:
        column_expert = (device * hidden_local + at + iota((1, size), 1)) // FF
        coef = jnp.where(column_expert == choices[0], first, jnp.where(column_expert == choices[1], second, 0.0))
        gate = dot_nt(moe_in, up_ref[0, at : at + size, :])
        up = dot_nt(moe_in, up_ref[1, at : at + size, :])
        hiddens.append((jax.nn.gelu(gate, approximate=True) * up * coef).astype(BF16))
    down_copy.wait()
    for (at, size), hidden in zip(chunks, hiddens):
        total = total + dot(hidden, down_ref[at : at + size, :])
    columns = total.shape[1] // 2
    for i in range(2):
        store_halves(total[:, i * columns : (i + 1) * columns], 1, sum_refs[i], sum_refs[2 + i])


def device_bits(axis):
    size = lax.axis_size(axis)
    assert size & (size - 1) == 0
    return [(axis, 1 << k) for k in range(size.bit_length() - 1)]


def swap(value, bit):
    axis, flip = bit
    return lax.ppermute(value, axis, [(i, i ^ flip) for i in range(lax.axis_size(axis))])


def reduce_halves(keep, give, split, bits):
    half = keep + swap(give, split)
    for bit in bits:
        half = half + swap(half, bit)
    return half, swap(half, split)


def reduce_columns(keeps, gives, split, orders):
    halves = [keep + swap(give, split) for keep, give in zip(keeps, gives)]
    for bits in zip(*orders):
        halves = [half + swap(half, bit) for half, bit in zip(halves, bits)]
    return halves, [swap(half, split) for half in halves]


def in_hbm(value):
    return pltpu.with_memory_space_constraint(value, pltpu.HBM)


def call(kernel, out_shape, in_specs, limit, scratch=()):
    shapes = [jax.ShapeDtypeStruct(shape, dtype) for shape, dtype in out_shape]
    return pl.pallas_call(
        kernel,
        out_shape=shapes,
        in_specs=in_specs,
        out_specs=[VMEM] * len(shapes),
        scratch_shapes=list(scratch),
        compiler_params=pltpu.CompilerParams(vmem_limit_bytes=limit << 20),
    )


def on_device(
    tokens_in,
    key_cache,
    value_cache,
    cache_len,
    bucket_table,
    rel_bias,
    attn_gain,
    moe_gain,
    w_qkv,
    w_out,
    router,
    expert_choice,
    w_gate_up,
    w_down,
):
    steps, requests, width = tokens_in.shape
    tokens = steps * requests
    half = tokens // 2
    _, cache_rows, features = key_cache.shape
    heads = features // HEAD_DIM
    rows = tokens * heads
    buckets = rel_bias.shape[0]
    hidden_local = w_down.shape[0]
    packed_shape = (tokens + 2 * heads, features)
    flat_in = tokens_in.reshape(tokens, width)
    dma = pltpu.SemaphoreType.DMA

    (packed,) = call(
        functools.partial(attend_kernel, steps, requests, heads),
        [(packed_shape, F32)],
        [HBM] * 8,
        16,
        [
            pltpu.SMEM(cache_len.shape, jnp.int32),
            pltpu.VMEM(flat_in.shape, BF16),
            pltpu.VMEM((1, width), F32),
            pltpu.VMEM((1,) + bucket_table.shape, jnp.int32),
            pltpu.VMEM((heads, buckets), F32),
            pltpu.VMEM(w_qkv.shape, BF16),
            pltpu.VMEM(key_cache.shape, BF16),
            pltpu.VMEM(value_cache.shape, BF16),
            pltpu.VMEM((rows, cache_rows), F32),
            pltpu.VMEM((rows, cache_rows), F32),
            pltpu.VMEM((rows, cache_rows), BF16),
            pltpu.VMEM((buckets, LANES), jnp.int32),
            pltpu.VMEM((buckets, steps * heads, LANES), F32),
            dma((5,)),
            dma((3,)),
            dma((requests // 4,)),
            dma((requests // 4,)),
        ],
    )(*map(in_hbm, (cache_len, flat_in, attn_gain, bucket_table, rel_bias.T, w_qkv, key_cache, value_cache)))

    packed, w_gate_up, w_down = lax.optimization_barrier((packed, w_gate_up, w_down))
    seq_bits, tp_bits = device_bits("seq"), device_bits("tp")
    for bit in seq_bits[:-1]:
        (packed,) = call(functools.partial(merge_kernel, tokens), [(packed_shape, F32)], [VMEM] * 2, 2)(
            packed, swap(packed, bit)
        )
    half_shape = ((half, width), F32)
    keep, give = call(
        functools.partial(project_kernel, steps, requests), [half_shape, half_shape], [VMEM] * 3, 4
    )(packed, swap(packed, seq_bits[-1]), w_out)

    mine, other = reduce_halves(keep, give, tp_bits[0], tp_bits[1:])

    column_shape = ((half, width // 2), F32)
    mid, *sums = call(expert_kernel, [((tokens, width), F32)] + [column_shape] * 4, [VMEM] * 7 + [HBM], 12, [pltpu.VMEM(w_down.shape, BF16), dma(())])(
        mine, other, flat_in, moe_gain[None], router.T, expert_choice.transpose(0, 2, 1), w_gate_up, in_hbm(w_down)
    )
    bits = tp_bits[1:] + seq_bits
    swapped = [bits[i ^ 1] if i ^ 1 < len(bits) else bits[i] for i in range(len(bits))]
    mine, other = reduce_columns(sums[:2], sums[2:], tp_bits[0], (bits, swapped))
    low = lax.axis_index("tp") % 2 == 0
    mine, other = jnp.concatenate(mine, axis=1), jnp.concatenate(other, axis=1)
    mixture = jnp.concatenate([jnp.where(low, mine, other), jnp.where(low, other, mine)])
    return (mid + mixture).astype(BF16).reshape(steps, requests, width)


def solution(mesh):
    return jax.shard_map(
        on_device,
        mesh=mesh,
        in_specs=(
            P(),
            P(None, "seq", "tp"),
            P(None, "seq", "tp"),
            P(),
            P(),
            P(None, "tp"),
            P(),
            P(),
            P(None, None, "tp"),
            P("tp", None),
            P(),
            P(),
            P(None, ("seq", "tp"), None),
            P(("seq", "tp"), None),
        ),
        out_specs=P(),
        check_vma=False,
    )
```

```python
import functools

import jax
import jax.numpy as jnp
from jax import lax
from jax.experimental import pallas as pl
from jax.experimental.pallas import tpu as pltpu
from jax.sharding import PartitionSpec as P

HEAD_DIM = 64
FF = 2816
LANES = 128
NEG = -1e30
EPS = 1e-06
F32 = jnp.float32
BF16 = jnp.bfloat16
VMEM = pl.BlockSpec(memory_space=pltpu.VMEM)
HBM = pl.BlockSpec(memory_space=pltpu.HBM)
NT = (((1,), (1,)), ((), ()))


def dot(one, two):
    return jnp.dot(one, two, preferred_element_type=F32)


def dot_nt(one, two):
    return lax.dot_general(one, two, NT, preferred_element_type=F32)


def iota(shape, dim):
    return lax.broadcasted_iota(jnp.int32, shape, dim)


def rms_scale(values, gain_vec):
    return values * lax.rsqrt(jnp.mean(values * values, axis=-1, keepdims=True) + EPS) * gain_vec


def shift_of(size):
    assert size & (size - 1) == 0
    return size.bit_length() - 1


def over(value, size):
    return lax.shift_right_logical(value, jnp.int32(shift_of(size)))


def modulo(value, size):
    assert size & (size - 1) == 0
    return value & (size - 1)


def attend_kernel(
    steps, requests, heads, len_hbm, tokens_hbm, gain_hbm, table_hbm, rel_hbm, w_hbm, k_hbm, v_hbm,
    out_ref, len_ref, tokens_ref, gain_ref, table_ref, rel_ref, w_buf, k_buf, v_buf,
    bias_buf, score_buf, weight_buf, start_buf, step_buf, small_sem, w_sem, k_sem, v_sem,
):
    tokens = steps * requests
    group = steps * heads
    rows = requests * group
    buckets = rel_ref.shape[1]
    cache_rows, features = k_buf.shape[1:]
    small = (
        (len_hbm, len_ref),
        (table_hbm, table_ref.at[0]),
        (rel_hbm, rel_ref),
        (tokens_hbm, tokens_ref),
        (gain_hbm, gain_ref.at[0]),
    )
    small_copies = [pltpu.make_async_copy(src, dst, small_sem.at[i]) for i, (src, dst) in enumerate(small)]
    w_copies = [pltpu.make_async_copy(w_hbm.at[k], w_buf.at[k], w_sem.at[k]) for k in range(3)]
    per_copy = requests // k_sem.shape[0]
    blocks = [pl.ds(i * per_copy, per_copy) for i in range(k_sem.shape[0])]
    k_copies = [pltpu.make_async_copy(k_hbm.at[b], k_buf.at[b], k_sem.at[i]) for i, b in enumerate(blocks)]
    v_copies = [pltpu.make_async_copy(v_hbm.at[b], v_buf.at[b], v_sem.at[i]) for i, b in enumerate(blocks)]
    for copy in small_copies + w_copies:
        copy.start()

    seq = lax.axis_index("seq")
    base = seq * cache_rows

    for copy in small_copies[:3]:
        copy.wait()
    table = table_ref[...]
    below = jnp.where(table < iota((buckets, table.shape[1]), 0), 1.0, 0.0)
    starts = jnp.sum(below, axis=1, keepdims=True).astype(jnp.int32)
    start_buf[...] = jnp.broadcast_to(starts, (buckets, LANES))

    group_head = over(iota((group, 1), 0), steps)
    level = jnp.zeros((group, buckets), F32)
    for h in range(heads):
        level = jnp.where(group_head == h, rel_ref[h : h + 1, :], level)
    for b in range(buckets):
        step_buf[b] = jnp.broadcast_to(level[:, b : b + 1], (group, LANES))

    def bias_of(pieces):
        width = pieces[0].shape[1]
        biases = [step_buf[0][:, :width]] * len(pieces)
        for b in range(1, buckets):
            start, value = start_buf[b : b + 1, :width], step_buf[b][:, :width]
            biases = [jnp.where(piece >= start, value, bias) for piece, bias in zip(pieces, biases)]
        return biases

    group_step = modulo(iota((group, 1), 0), steps)
    col_slices = [slice(c, c + LANES) for c in range(0, cache_rows, LANES)]
    offsets = [group_step - iota((1, LANES), 1) - (base + c.start) for c in col_slices]
    per_trip = 2

    def fill_bias(trip, carry):
        places, distances = [], []
        for i in range(per_trip):
            r = trip * per_trip + i
            length = len_ref[r]
            for cols, offset in zip(col_slices, offsets):
                places.append((pl.ds(pl.multiple_of(r * group, group), group), cols))
                distances.append(offset + length)
        for place, distance, bias in zip(places, distances, bias_of(distances)):
            bias_buf[place] = jnp.where(distance > group_step, bias, NEG)
        return carry

    for copy in k_copies:
        copy.start()
    lax.fori_loop(0, requests // per_trip, fill_bias, 0)
    for copy in v_copies:
        copy.start()

    for copy in small_copies[3:]:
        copy.wait()
    x = tokens_ref[...].astype(F32)
    normed = rms_scale(x, gain_ref[...]).astype(BF16)
    projected = []
    for k in range(3):
        w_copies[k].wait()
        projected.append(dot(normed, w_buf[k]).astype(BF16))
    queries, fresh_keys, fresh_values = projected

    row = iota((rows, 1), 0)
    row_step, row_head, row_request = modulo(row, steps), modulo(over(row, steps), heads), over(row, group)
    column = iota((1, tokens), 1)
    pick = jnp.where(row_step * requests + row_request == column, 1.0, 0.0).astype(BF16)
    own_head = row_head == over(iota((1, features), 1), HEAD_DIM)
    spread = jnp.where(own_head, dot(pick, queries), 0.0).astype(BF16)

    key_step, key_request = over(column, requests), modulo(column, requests)
    newest = jnp.where(seq == 0, row_step, -1)
    fresh_live = jnp.logical_and(key_step <= newest, key_request == row_request)
    (fresh_bias,) = bias_of([group_step - key_step])
    fresh_bias = jnp.concatenate([fresh_bias] * requests, axis=0)
    fresh_scores = jnp.where(fresh_live, dot_nt(spread, fresh_keys) + fresh_bias, NEG)

    for copy in k_copies:
        copy.wait()
    for r in range(requests):
        at = slice(r * group, (r + 1) * group)
        score_buf[at, :] = dot_nt(spread[at], k_buf[r])
    scores = score_buf[...] + bias_buf[...]
    top = jnp.maximum(jnp.max(scores, axis=1, keepdims=True), jnp.max(fresh_scores, axis=1, keepdims=True))
    weights = jnp.where(scores > 0.5 * NEG, jnp.exp(scores - top), 0.0)
    fresh_weights = jnp.where(fresh_live, jnp.exp(fresh_scores - top), 0.0)
    total = jnp.sum(weights, axis=1, keepdims=True) + jnp.sum(fresh_weights, axis=1, keepdims=True)
    weight_buf[...] = weights.astype(BF16)
    score_buf[...] = dot(fresh_weights.astype(BF16), fresh_values)
    for copy in v_copies:
        copy.wait()

    lane = iota((1, LANES), 1)
    stats = jnp.where(lane == row_head, top, jnp.where(lane == heads + row_head, total, 0.0))
    group_own = own_head[:group]
    first = iota((8, 1), 0) < steps

    def folded(part):
        half = part[:8] + part[8:]
        return half + pltpu.roll(half, steps, 0)

    stat_pairs = []
    for pair in range(requests // 2):
        sums, stat_parts = [], []
        for r in (2 * pair, 2 * pair + 1):
            at = slice(r * group, (r + 1) * group)
            sums.append(folded(jnp.where(group_own, dot(weight_buf[at, :], v_buf[r]) + score_buf[at, :], 0.0)))
            stat_parts.append(folded(stats[at]))
        out_ref[8 * pair : 8 * pair + 8, :] = jnp.where(first, sums[0], sums[1])
        stat_pairs.append(jnp.where(first, stat_parts[0], stat_parts[1]))
    out_ref[tokens:, :] = jnp.zeros((2 * heads, features), F32)
    out_ref[tokens:, :LANES] = turned(jnp.concatenate(stat_pairs, axis=0))[: 2 * heads]


def turned(value):
    rows = value.shape[0]
    if rows < LANES:
        value = jnp.concatenate([value, jnp.zeros((LANES - rows, LANES), F32)], axis=0)
    return value.T


def widen(columns, first, heads):
    lane_head = over(iota((1, heads * HEAD_DIM), 1), HEAD_DIM)
    wide = jnp.broadcast_to(columns[:, first : first + 1], (columns.shape[0], heads * HEAD_DIM))
    for h in range(1, heads):
        wide = jnp.where(lane_head == h, columns[:, first + h : first + h + 1], wide)
    return wide


def tree(operation, values):
    while len(values) > 1:
        values = [operation(*values[i : i + 2]) for i in range(0, len(values), 2)]
    return values[0]


def merge_parts(tokens, parts):
    heads = parts[0].shape[1] // HEAD_DIM
    stats = [part[tokens:, :LANES] for part in parts]
    top = tree(jnp.maximum, stats)
    scales = [jnp.exp(stat - top) for stat in stats]
    totals = tree(jnp.add, [stat * pltpu.roll(scale, heads, 0) for stat, scale in zip(stats, scales)])
    stat = jnp.where(iota((2 * heads, 1), 0) < heads, top, totals)
    columns = turned(jnp.concatenate(scales + [stat], axis=0))[:tokens]
    sums = tree(
        jnp.add, [part[:tokens, :] * widen(columns, 2 * heads * i, heads) for i, part in enumerate(parts)]
    )
    return sums, stat, widen(columns, 2 * heads * len(parts) + heads, heads)


def merge_kernel(tokens, one_ref, two_ref, _, out_ref):
    sums, stat, _ = merge_parts(tokens, (one_ref, two_ref))
    out_ref[:tokens, :] = sums
    out_ref[tokens:, :] = jnp.zeros((stat.shape[0], sums.shape[1]), F32)
    out_ref[tokens:, :LANES] = stat


def store_halves(value, bit, keep_ref, give_ref):
    half = value.shape[0] // 2
    low = lax.axis_index("tp") // bit % 2 == 0
    keep_ref[...] = jnp.where(low, value[:half], value[half:])
    give_ref[...] = jnp.where(low, value[half:], value[:half])


def project_kernel(steps, requests, one_ref, two_ref, w_ref, _, keep_ref, give_ref):
    tokens = steps * requests
    sums, _, totals = merge_parts(tokens, (one_ref, two_ref))
    attended = (sums / totals).astype(BF16)
    row = iota((tokens, 1), 0)
    source = modulo(row, requests) * steps + over(row, requests)
    order = jnp.where(source == iota((1, tokens), 1), 1.0, 0.0).astype(BF16)
    attended = dot(order, attended).astype(BF16)
    store_halves(dot(attended, w_ref[...]), 1, keep_ref, give_ref)


def chunks_of(total, size):
    return [(at, min(size, total - at)) for at in range(0, total, size)]


def add_kernel(one_ref, two_ref, _, out_ref):
    out_ref[...] = one_ref[...] + two_ref[...]


def fetch_kernel(index, after_ref, weights_hbm, out_ref, done_ref, sems):
    del after_ref
    source = weights_hbm if index is None else weights_hbm.at[index]
    copies = []
    for i, (at, size) in enumerate(chunks_of(out_ref.shape[0], 384)):
        rows = pl.ds(at, size)
        copies.append(pltpu.make_async_copy(source.at[rows], out_ref.at[rows], sems.at[i]))
        copies[-1].start()
    done_ref[...] = jnp.zeros_like(done_ref)
    for copy in copies:
        copy.wait()


def fetch(after, weights, index=None):
    shape = weights.shape[-2:]
    return call(
        functools.partial(fetch_kernel, index),
        [(shape, BF16), ((8, LANES), F32)],
        [VMEM, HBM],
        1,
        [pltpu.SemaphoreType.DMA((len(chunks_of(shape[0], 384)),))],
    )(after, in_hbm(weights))


def expert_kernel(
    half_ref, back_ref, tokens_ref, gain_ref, router_ref, choice_ref, gate_ref, up_ref, down_ref, mid_ref, *sum_refs
):
    hidden_local = down_ref.shape[0]
    half = half_ref.shape[0]
    steps, _, requests = choice_ref.shape
    low = lax.axis_index("tp") % 2 == 0
    mine, other = half_ref[...], back_ref[...]
    mid_ref[:half] = tokens_ref[:half].astype(F32) + jnp.where(low, mine, other)
    mid_ref[half:] = tokens_ref[half:].astype(F32) + jnp.where(low, other, mine)
    moe_in = rms_scale(mid_ref[...], gain_ref[...]).astype(BF16)
    logits = dot_nt(moe_in, router_ref[...])
    expert = iota((1, logits.shape[1]), 1)
    own = iota((requests, 1), 0) == iota((1, requests), 1)
    choices, chosen = [], []
    for pick in range(2):
        column = [
            jnp.sum(jnp.where(own, choice_ref[t, pick : pick + 1, :].astype(F32), 0.0), axis=1, keepdims=True)
            for t in range(steps)
        ]
        choices.append(jnp.concatenate(column, axis=0).astype(jnp.int32))
        chosen.append(jnp.sum(jnp.where(expert == choices[pick], logits, 0.0), axis=1, keepdims=True))
    first = 1.0 / (1.0 + jnp.exp(chosen[1] - chosen[0]))
    second = 1.0 - first
    device = lax.axis_index("seq") * lax.axis_size("tp") + lax.axis_index("tp")
    total = jnp.zeros(mid_ref.shape, F32)
    for at, size in chunks_of(hidden_local, 256):
        column_expert = (device * hidden_local + at + iota((1, size), 1)) // FF
        coef = jnp.where(column_expert == choices[0], first, jnp.where(column_expert == choices[1], second, 0.0))
        gate = dot_nt(moe_in, gate_ref[at : at + size, :])
        up = dot_nt(moe_in, up_ref[at : at + size, :])
        hidden = (jax.nn.gelu(gate, approximate=True) * up * coef).astype(BF16)
        total = total + dot(hidden, down_ref[at : at + size, :])
    columns = total.shape[1] // 2
    for i in range(2):
        store_halves(total[:, i * columns : (i + 1) * columns], 1, sum_refs[i], sum_refs[2 + i])


def device_bits(axis):
    size = lax.axis_size(axis)
    assert size & (size - 1) == 0
    return [(axis, 1 << k) for k in range(size.bit_length() - 1)]


def swap(value, bit):
    axis, flip = bit
    return lax.ppermute(value, axis, [(i, i ^ flip) for i in range(lax.axis_size(axis))])


def reduce_columns(keeps, gives, split, orders):
    halves = [keep + swap(give, split) for keep, give in zip(keeps, gives)]
    for bits in zip(*orders):
        halves = [half + swap(half, bit) for half, bit in zip(halves, bits)]
    return halves, [swap(half, split) for half in halves]


def in_hbm(value):
    return pltpu.with_memory_space_constraint(value, pltpu.HBM)


def call(kernel, out_shape, in_specs, limit, scratch=()):
    shapes = [jax.ShapeDtypeStruct(shape, dtype) for shape, dtype in out_shape]
    return pl.pallas_call(
        kernel,
        out_shape=shapes,
        in_specs=in_specs,
        out_specs=[VMEM] * len(shapes),
        scratch_shapes=list(scratch),
        compiler_params=pltpu.CompilerParams(vmem_limit_bytes=limit << 20),
    )


def on_device(
    tokens_in,
    key_cache,
    value_cache,
    cache_len,
    bucket_table,
    rel_bias,
    attn_gain,
    moe_gain,
    w_qkv,
    w_out,
    router,
    expert_choice,
    w_gate_up,
    w_down,
):
    steps, requests, width = tokens_in.shape
    tokens = steps * requests
    half = tokens // 2
    _, cache_rows, features = key_cache.shape
    heads = features // HEAD_DIM
    rows = tokens * heads
    buckets = rel_bias.shape[0]
    hidden_local = w_down.shape[0]
    packed_shape = (tokens + 2 * heads, features)
    flat_in = tokens_in.reshape(tokens, width)
    dma = pltpu.SemaphoreType.DMA

    (packed,) = call(
        functools.partial(attend_kernel, steps, requests, heads),
        [(packed_shape, F32)],
        [HBM] * 8,
        16,
        [
            pltpu.SMEM(cache_len.shape, jnp.int32),
            pltpu.VMEM(flat_in.shape, BF16),
            pltpu.VMEM((1, width), F32),
            pltpu.VMEM((1,) + bucket_table.shape, jnp.int32),
            pltpu.VMEM((heads, buckets), F32),
            pltpu.VMEM(w_qkv.shape, BF16),
            pltpu.VMEM(key_cache.shape, BF16),
            pltpu.VMEM(value_cache.shape, BF16),
            pltpu.VMEM((rows, cache_rows), F32),
            pltpu.VMEM((rows, cache_rows), F32),
            pltpu.VMEM((rows, cache_rows), BF16),
            pltpu.VMEM((buckets, LANES), jnp.int32),
            pltpu.VMEM((buckets, steps * heads, LANES), F32),
            dma((5,)),
            dma((3,)),
            dma((requests // 4,)),
            dma((requests // 4,)),
        ],
    )(*map(in_hbm, (cache_len, flat_in, attn_gain, bucket_table, rel_bias.T, w_qkv, key_cache, value_cache)))

    seq_bits, tp_bits = device_bits("seq"), device_bits("tp")
    staged = []
    token = jnp.zeros((8, LANES), F32)
    for i, bit in enumerate(seq_bits):
        other = swap(packed, bit)
        if i >= len(seq_bits) - 2:
            weights, token = fetch(packed, w_gate_up, len(staged))
            staged.append(weights)
        if i < len(seq_bits) - 1:
            (packed,) = call(functools.partial(merge_kernel, tokens), [(packed_shape, F32)], [VMEM] * 3, 2)(
                packed, other, token
            )
    half_shape = ((half, width), F32)
    keep, give = call(
        functools.partial(project_kernel, steps, requests), [half_shape, half_shape], [VMEM] * 4, 4
    )(packed, other, w_out, token)

    half_sum = keep + swap(give, tp_bits[0])
    for bit in tp_bits[1:]:
        other = swap(half_sum, bit)
        if len(staged) == 2:
            weights, token = fetch(half_sum, w_down)
            staged.append(weights)
        (half_sum,) = call(add_kernel, [half_shape], [VMEM] * 3, 1)(half_sum, other, token)
    mine, other = half_sum, swap(half_sum, tp_bits[0])

    column_shape = ((half, width // 2), F32)
    mid, *sums = call(expert_kernel, [((tokens, width), F32)] + [column_shape] * 4, [VMEM] * 9, 8)(
        mine, other, flat_in, moe_gain[None], router.T, expert_choice.transpose(0, 2, 1), *staged
    )
    bits = tp_bits[1:] + seq_bits
    swapped = [bits[i ^ 1] if i ^ 1 < len(bits) else bits[i] for i in range(len(bits))]
    mine, other = reduce_columns(sums[:2], sums[2:], tp_bits[0], (bits, swapped))
    low = lax.axis_index("tp") % 2 == 0
    mine, other = jnp.concatenate(mine, axis=1), jnp.concatenate(other, axis=1)
    mixture = jnp.concatenate([jnp.where(low, mine, other), jnp.where(low, other, mine)])
    return (mid + mixture).astype(BF16).reshape(steps, requests, width)


def solution(mesh):
    return jax.shard_map(
        on_device,
        mesh=mesh,
        in_specs=(
            P(),
            P(None, "seq", "tp"),
            P(None, "seq", "tp"),
            P(),
            P(),
            P(None, "tp"),
            P(),
            P(),
            P(None, None, "tp"),
            P("tp", None),
            P(),
            P(),
            P(None, ("seq", "tp"), None),
            P(("seq", "tp"), None),
        ),
        out_specs=P(),
        check_vma=False,
    )
```

```python
import functools

import jax
import jax.numpy as jnp
from jax import lax
from jax.experimental import pallas as pl
from jax.experimental.pallas import tpu as pltpu
from jax.sharding import PartitionSpec as P

HEAD_DIM = 64
FF = 2816
LANES = 128
NEG = -1e30
EPS = 1e-06
F32 = jnp.float32
BF16 = jnp.bfloat16
VMEM = pl.BlockSpec(memory_space=pltpu.VMEM)
HBM = pl.BlockSpec(memory_space=pltpu.HBM)
NT = (((1,), (1,)), ((), ()))


def dot(one, two):
    return jnp.dot(one, two, preferred_element_type=F32)


def dot_nt(one, two):
    return lax.dot_general(one, two, NT, preferred_element_type=F32)


def iota(shape, dim):
    return lax.broadcasted_iota(jnp.int32, shape, dim)


def rms_scale(values, gain_vec):
    return values * lax.rsqrt(jnp.mean(values * values, axis=-1, keepdims=True) + EPS) * gain_vec


def shift_of(size):
    assert size & (size - 1) == 0
    return size.bit_length() - 1


def over(value, size):
    return lax.shift_right_logical(value, jnp.int32(shift_of(size)))


def modulo(value, size):
    assert size & (size - 1) == 0
    return value & (size - 1)


def attend_kernel(
    steps, requests, heads, len_hbm, tokens_hbm, gain_hbm, table_hbm, rel_hbm, w_hbm, k_hbm, v_hbm,
    out_ref, len_ref, tokens_ref, gain_ref, table_ref, rel_ref, w_buf, k_buf, v_buf,
    bias_buf, score_buf, weight_buf, start_buf, step_buf, small_sem, w_sem, k_sem, v_sem,
):
    tokens = steps * requests
    group = steps * heads
    rows = requests * group
    buckets = rel_ref.shape[1]
    cache_rows, features = k_buf.shape[1:]
    small = (
        (len_hbm, len_ref),
        (table_hbm, table_ref.at[0]),
        (rel_hbm, rel_ref),
        (tokens_hbm, tokens_ref),
        (gain_hbm, gain_ref.at[0]),
    )
    small_copies = [pltpu.make_async_copy(src, dst, small_sem.at[i]) for i, (src, dst) in enumerate(small)]
    w_copies = [pltpu.make_async_copy(w_hbm.at[k], w_buf.at[k], w_sem.at[k]) for k in range(3)]
    per_copy = requests // k_sem.shape[0]
    blocks = [pl.ds(i * per_copy, per_copy) for i in range(k_sem.shape[0])]
    k_copies = [pltpu.make_async_copy(k_hbm.at[b], k_buf.at[b], k_sem.at[i]) for i, b in enumerate(blocks)]
    v_copies = [pltpu.make_async_copy(v_hbm.at[b], v_buf.at[b], v_sem.at[i]) for i, b in enumerate(blocks)]
    for copy in small_copies + w_copies:
        copy.start()

    seq = lax.axis_index("seq")
    base = seq * cache_rows

    for copy in small_copies[:3]:
        copy.wait()
    table = table_ref[...]
    below = jnp.where(table < iota((buckets, table.shape[1]), 0), 1.0, 0.0)
    starts = jnp.sum(below, axis=1, keepdims=True).astype(jnp.int32)
    start_buf[...] = jnp.broadcast_to(starts, (buckets, LANES))

    group_head = over(iota((group, 1), 0), steps)
    level = jnp.zeros((group, buckets), F32)
    for h in range(heads):
        level = jnp.where(group_head == h, rel_ref[h : h + 1, :], level)
    for b in range(buckets):
        step_buf[b] = jnp.broadcast_to(level[:, b : b + 1], (group, LANES))

    def bias_of(pieces):
        width = pieces[0].shape[1]
        biases = [step_buf[0][:, :width]] * len(pieces)
        for b in range(1, buckets):
            start, value = start_buf[b : b + 1, :width], step_buf[b][:, :width]
            biases = [jnp.where(piece >= start, value, bias) for piece, bias in zip(pieces, biases)]
        return biases

    group_step = modulo(iota((group, 1), 0), steps)
    col_slices = [slice(c, c + LANES) for c in range(0, cache_rows, LANES)]
    offsets = [group_step - iota((1, LANES), 1) - (base + c.start) for c in col_slices]
    per_trip = 2

    def fill_bias(trip, carry):
        places, distances = [], []
        for i in range(per_trip):
            r = trip * per_trip + i
            length = len_ref[r]
            for cols, offset in zip(col_slices, offsets):
                places.append((pl.ds(pl.multiple_of(r * group, group), group), cols))
                distances.append(offset + length)
        for place, distance, bias in zip(places, distances, bias_of(distances)):
            bias_buf[place] = jnp.where(distance > group_step, bias, NEG)
        return carry

    for copy in k_copies:
        copy.start()
    lax.fori_loop(0, requests // per_trip, fill_bias, 0)
    for copy in v_copies:
        copy.start()

    for copy in small_copies[3:]:
        copy.wait()
    x = tokens_ref[...].astype(F32)
    normed = rms_scale(x, gain_ref[...]).astype(BF16)
    projected = []
    for k in range(3):
        w_copies[k].wait()
        projected.append(dot(normed, w_buf[k]).astype(BF16))
    queries, fresh_keys, fresh_values = projected

    row = iota((rows, 1), 0)
    row_step, row_head, row_request = modulo(row, steps), modulo(over(row, steps), heads), over(row, group)
    column = iota((1, tokens), 1)
    pick = jnp.where(row_step * requests + row_request == column, 1.0, 0.0).astype(BF16)
    own_head = row_head == over(iota((1, features), 1), HEAD_DIM)
    spread = jnp.where(own_head, dot(pick, queries), 0.0).astype(BF16)

    key_step, key_request = over(column, requests), modulo(column, requests)
    newest = jnp.where(seq == 0, row_step, -1)
    fresh_live = jnp.logical_and(key_step <= newest, key_request == row_request)
    (fresh_bias,) = bias_of([group_step - key_step])
    fresh_bias = jnp.concatenate([fresh_bias] * requests, axis=0)
    fresh_scores = jnp.where(fresh_live, dot_nt(spread, fresh_keys) + fresh_bias, NEG)

    for copy in k_copies:
        copy.wait()
    for r in range(requests):
        at = slice(r * group, (r + 1) * group)
        score_buf[at, :] = dot_nt(spread[at], k_buf[r])
    scores = score_buf[...] + bias_buf[...]
    top = jnp.maximum(jnp.max(scores, axis=1, keepdims=True), jnp.max(fresh_scores, axis=1, keepdims=True))
    weights = jnp.where(scores > 0.5 * NEG, jnp.exp(scores - top), 0.0)
    fresh_weights = jnp.where(fresh_live, jnp.exp(fresh_scores - top), 0.0)
    total = jnp.sum(weights, axis=1, keepdims=True) + jnp.sum(fresh_weights, axis=1, keepdims=True)
    weight_buf[...] = weights.astype(BF16)
    score_buf[...] = dot(fresh_weights.astype(BF16), fresh_values)
    for copy in v_copies:
        copy.wait()

    lane = iota((1, LANES), 1)
    stats = jnp.where(lane == row_head, top, jnp.where(lane == heads + row_head, total, 0.0))
    group_own = own_head[:group]
    first = iota((8, 1), 0) < steps

    def folded(part):
        half = part[:8] + part[8:]
        return half + pltpu.roll(half, steps, 0)

    stat_pairs = []
    for pair in range(requests // 2):
        sums, stat_parts = [], []
        for r in (2 * pair, 2 * pair + 1):
            at = slice(r * group, (r + 1) * group)
            sums.append(folded(jnp.where(group_own, dot(weight_buf[at, :], v_buf[r]) + score_buf[at, :], 0.0)))
            stat_parts.append(folded(stats[at]))
        out_ref[8 * pair : 8 * pair + 8, :] = jnp.where(first, sums[0], sums[1])
        stat_pairs.append(jnp.where(first, stat_parts[0], stat_parts[1]))
    out_ref[tokens:, :] = jnp.zeros((2 * heads, features), F32)
    out_ref[tokens:, :LANES] = turned(jnp.concatenate(stat_pairs, axis=0))[: 2 * heads]


def turned(value):
    rows = value.shape[0]
    if rows < LANES:
        value = jnp.concatenate([value, jnp.zeros((LANES - rows, LANES), F32)], axis=0)
    return value.T


def widen(columns, first, heads):
    lane_head = over(iota((1, heads * HEAD_DIM), 1), HEAD_DIM)
    wide = jnp.broadcast_to(columns[:, first : first + 1], (columns.shape[0], heads * HEAD_DIM))
    for h in range(1, heads):
        wide = jnp.where(lane_head == h, columns[:, first + h : first + h + 1], wide)
    return wide


def tree(operation, values):
    while len(values) > 1:
        values = [operation(*values[i : i + 2]) for i in range(0, len(values), 2)]
    return values[0]


def merge_parts(tokens, parts):
    heads = parts[0].shape[1] // HEAD_DIM
    stats = [part[tokens:, :LANES] for part in parts]
    top = tree(jnp.maximum, stats)
    scales = [jnp.exp(stat - top) for stat in stats]
    totals = tree(jnp.add, [stat * pltpu.roll(scale, heads, 0) for stat, scale in zip(stats, scales)])
    stat = jnp.where(iota((2 * heads, 1), 0) < heads, top, totals)
    columns = turned(jnp.concatenate(scales + [stat], axis=0))[:tokens]
    sums = tree(
        jnp.add, [part[:tokens, :] * widen(columns, 2 * heads * i, heads) for i, part in enumerate(parts)]
    )
    return sums, stat, widen(columns, 2 * heads * len(parts) + heads, heads)


def merge_kernel(tokens, one_ref, two_ref, _, out_ref):
    sums, stat, _ = merge_parts(tokens, (one_ref, two_ref))
    out_ref[:tokens, :] = sums
    out_ref[tokens:, :] = jnp.zeros((stat.shape[0], sums.shape[1]), F32)
    out_ref[tokens:, :LANES] = stat


def store_halves(value, bit, keep_ref, give_ref):
    half = value.shape[0] // 2
    low = lax.axis_index("tp") // bit % 2 == 0
    keep_ref[...] = jnp.where(low, value[:half], value[half:])
    give_ref[...] = jnp.where(low, value[half:], value[:half])


def project_kernel(steps, requests, one_ref, two_ref, w_ref, _, keep_ref, give_ref):
    tokens = steps * requests
    sums, _, totals = merge_parts(tokens, (one_ref, two_ref))
    attended = (sums / totals).astype(BF16)
    row = iota((tokens, 1), 0)
    source = modulo(row, requests) * steps + over(row, requests)
    order = jnp.where(source == iota((1, tokens), 1), 1.0, 0.0).astype(BF16)
    attended = dot(order, attended).astype(BF16)
    store_halves(dot(attended, w_ref[...]), 1, keep_ref, give_ref)


def chunks_of(total, size):
    return [(at, min(size, total - at)) for at in range(0, total, size)]


def add_kernel(one_ref, two_ref, _, out_ref):
    out_ref[...] = one_ref[...] + two_ref[...]


def fetch_kernel(index, after_ref, weights_hbm, out_ref, done_ref, sems):
    del after_ref
    source = weights_hbm if index is None else weights_hbm.at[index]
    copies = []
    for i, (at, size) in enumerate(chunks_of(out_ref.shape[0], 384)):
        rows = pl.ds(at, size)
        copies.append(pltpu.make_async_copy(source.at[rows], out_ref.at[rows], sems.at[i]))
        copies[-1].start()
    done_ref[...] = jnp.zeros_like(done_ref)
    for copy in copies:
        copy.wait()


def fetch(after, weights, index=None):
    shape = weights.shape[-2:]
    return call(
        functools.partial(fetch_kernel, index),
        [(shape, BF16), ((8, LANES), F32)],
        [VMEM, HBM],
        1,
        [pltpu.SemaphoreType.DMA((len(chunks_of(shape[0], 384)),))],
    )(after, in_hbm(weights))


def expert_kernel(
    half_ref, back_ref, tokens_ref, gain_ref, router_ref, choice_ref, gate_ref, up_ref, down_ref,
    mid_ref, hidden_ref, keep_ref, give_ref,
):
    hidden_local = down_ref.shape[0]
    half = half_ref.shape[0]
    steps, _, requests = choice_ref.shape
    low = lax.axis_index("tp") % 2 == 0
    mine, other = half_ref[...], back_ref[...]
    mid_ref[:half] = tokens_ref[:half].astype(F32) + jnp.where(low, mine, other)
    mid_ref[half:] = tokens_ref[half:].astype(F32) + jnp.where(low, other, mine)
    moe_in = rms_scale(mid_ref[...], gain_ref[...]).astype(BF16)
    logits = dot_nt(moe_in, router_ref[...])
    expert = iota((1, logits.shape[1]), 1)
    own = iota((requests, 1), 0) == iota((1, requests), 1)
    choices, chosen = [], []
    for pick in range(2):
        column = [
            jnp.sum(jnp.where(own, choice_ref[t, pick : pick + 1, :].astype(F32), 0.0), axis=1, keepdims=True)
            for t in range(steps)
        ]
        choices.append(jnp.concatenate(column, axis=0).astype(jnp.int32))
        chosen.append(jnp.sum(jnp.where(expert == choices[pick], logits, 0.0), axis=1, keepdims=True))
    first = 1.0 / (1.0 + jnp.exp(chosen[1] - chosen[0]))
    second = 1.0 - first
    device = lax.axis_index("seq") * lax.axis_size("tp") + lax.axis_index("tp")
    column_expert = (device * hidden_local + iota((1, hidden_local), 1)) // FF
    coef = jnp.where(column_expert == choices[0], first, jnp.where(column_expert == choices[1], second, 0.0))
    gate = dot_nt(moe_in, gate_ref[...])
    up = dot_nt(moe_in, up_ref[...])
    hidden = (jax.nn.gelu(gate, approximate=True) * up * coef).astype(BF16)
    hidden_ref[...] = hidden
    store_halves(dot(hidden, down_ref[:, : keep_ref.shape[1]]), 1, keep_ref, give_ref)


def down_kernel(hidden_ref, down_ref, keep_ref, give_ref):
    store_halves(dot(hidden_ref[...], down_ref[:, keep_ref.shape[1] :]), 1, keep_ref, give_ref)


def device_bits(axis):
    size = lax.axis_size(axis)
    assert size & (size - 1) == 0
    return [(axis, 1 << k) for k in range(size.bit_length() - 1)]


def swap(value, bit):
    axis, flip = bit
    return lax.ppermute(value, axis, [(i, i ^ flip) for i in range(lax.axis_size(axis))])


def reduce_columns(halves, split, orders):
    for bits in zip(*orders):
        halves = [half + swap(half, bit) for half, bit in zip(halves, bits)]
    return halves, [swap(half, split) for half in halves]


def in_hbm(value):
    return pltpu.with_memory_space_constraint(value, pltpu.HBM)


def call(kernel, out_shape, in_specs, limit, scratch=()):
    shapes = [jax.ShapeDtypeStruct(shape, dtype) for shape, dtype in out_shape]
    return pl.pallas_call(
        kernel,
        out_shape=shapes,
        in_specs=in_specs,
        out_specs=[VMEM] * len(shapes),
        scratch_shapes=list(scratch),
        compiler_params=pltpu.CompilerParams(vmem_limit_bytes=limit << 20),
    )


def on_device(
    tokens_in,
    key_cache,
    value_cache,
    cache_len,
    bucket_table,
    rel_bias,
    attn_gain,
    moe_gain,
    w_qkv,
    w_out,
    router,
    expert_choice,
    w_gate_up,
    w_down,
):
    steps, requests, width = tokens_in.shape
    tokens = steps * requests
    half = tokens // 2
    _, cache_rows, features = key_cache.shape
    heads = features // HEAD_DIM
    rows = tokens * heads
    buckets = rel_bias.shape[0]
    hidden_local = w_down.shape[0]
    packed_shape = (tokens + 2 * heads, features)
    flat_in = tokens_in.reshape(tokens, width)
    dma = pltpu.SemaphoreType.DMA

    (packed,) = call(
        functools.partial(attend_kernel, steps, requests, heads),
        [(packed_shape, F32)],
        [HBM] * 8,
        16,
        [
            pltpu.SMEM(cache_len.shape, jnp.int32),
            pltpu.VMEM(flat_in.shape, BF16),
            pltpu.VMEM((1, width), F32),
            pltpu.VMEM((1,) + bucket_table.shape, jnp.int32),
            pltpu.VMEM((heads, buckets), F32),
            pltpu.VMEM(w_qkv.shape, BF16),
            pltpu.VMEM(key_cache.shape, BF16),
            pltpu.VMEM(value_cache.shape, BF16),
            pltpu.VMEM((rows, cache_rows), F32),
            pltpu.VMEM((rows, cache_rows), F32),
            pltpu.VMEM((rows, cache_rows), BF16),
            pltpu.VMEM((buckets, LANES), jnp.int32),
            pltpu.VMEM((buckets, steps * heads, LANES), F32),
            dma((5,)),
            dma((3,)),
            dma((requests // 4,)),
            dma((requests // 4,)),
        ],
    )(*map(in_hbm, (cache_len, flat_in, attn_gain, bucket_table, rel_bias.T, w_qkv, key_cache, value_cache)))

    seq_bits, tp_bits = device_bits("seq"), device_bits("tp")
    staged = []
    token = jnp.zeros((8, LANES), F32)
    for i, bit in enumerate(seq_bits):
        other = swap(packed, bit)
        if i >= len(seq_bits) - 2:
            weights, token = fetch(packed, w_gate_up, len(staged))
            staged.append(weights)
        if i < len(seq_bits) - 1:
            (packed,) = call(functools.partial(merge_kernel, tokens), [(packed_shape, F32)], [VMEM] * 3, 2)(
                packed, other, token
            )
    half_shape = ((half, width), F32)
    keep, give = call(
        functools.partial(project_kernel, steps, requests), [half_shape, half_shape], [VMEM] * 4, 4
    )(packed, other, w_out, token)

    half_sum = keep + swap(give, tp_bits[0])
    for bit in tp_bits[1:]:
        other = swap(half_sum, bit)
        if len(staged) == 2:
            weights, token = fetch(half_sum, w_down)
            staged.append(weights)
        (half_sum,) = call(add_kernel, [half_shape], [VMEM] * 3, 1)(half_sum, other, token)
    mine, other = half_sum, swap(half_sum, tp_bits[0])

    column_shape = ((half, width // 2), F32)
    expert_shapes = [((tokens, width), F32), ((tokens, hidden_local), BF16), column_shape, column_shape]
    mid, hidden, keep, give = call(expert_kernel, expert_shapes, [VMEM] * 9, 8)(
        mine, other, flat_in, moe_gain[None], router.T, expert_choice.transpose(0, 2, 1), *staged
    )
    back = swap(give, tp_bits[0])
    keep_two, give_two = call(down_kernel, [column_shape] * 2, [VMEM] * 2, 4)(hidden, staged[2])
    blocks = [keep + back, keep_two + swap(give_two, tp_bits[0])]
    bits = tp_bits[1:] + seq_bits
    swapped = [bits[i ^ 1] if i ^ 1 < len(bits) else bits[i] for i in range(len(bits))]
    mine, other = reduce_columns(blocks, tp_bits[0], (bits, swapped))
    low = lax.axis_index("tp") % 2 == 0
    mine, other = jnp.concatenate(mine, axis=1), jnp.concatenate(other, axis=1)
    mixture = jnp.concatenate([jnp.where(low, mine, other), jnp.where(low, other, mine)])
    return (mid + mixture).astype(BF16).reshape(steps, requests, width)


def solution(mesh):
    return jax.shard_map(
        on_device,
        mesh=mesh,
        in_specs=(
            P(),
            P(None, "seq", "tp"),
            P(None, "seq", "tp"),
            P(),
            P(),
            P(None, "tp"),
            P(),
            P(),
            P(None, None, "tp"),
            P("tp", None),
            P(),
            P(),
            P(None, ("seq", "tp"), None),
            P(("seq", "tp"), None),
        ),
        out_specs=P(),
        check_vma=False,
    )
```

```python
import functools

import jax
import jax.numpy as jnp
from jax import lax
from jax.experimental import pallas as pl
from jax.experimental.pallas import tpu as pltpu
from jax.sharding import PartitionSpec as P

HEAD_DIM = 64
FF = 2816
LANES = 128
NEG = -1e30
EPS = 1e-06
F32 = jnp.float32
BF16 = jnp.bfloat16
VMEM = pl.BlockSpec(memory_space=pltpu.VMEM)
HBM = pl.BlockSpec(memory_space=pltpu.HBM)
NT = (((1,), (1,)), ((), ()))


def dot(one, two):
    return jnp.dot(one, two, preferred_element_type=F32)


def dot_nt(one, two):
    return lax.dot_general(one, two, NT, preferred_element_type=F32)


def iota(shape, dim):
    return lax.broadcasted_iota(jnp.int32, shape, dim)


def rms_scale(values, gain_vec):
    return values * lax.rsqrt(jnp.mean(values * values, axis=-1, keepdims=True) + EPS) * gain_vec


def shift_of(size):
    assert size & (size - 1) == 0
    return size.bit_length() - 1


def over(value, size):
    return lax.shift_right_logical(value, jnp.int32(shift_of(size)))


def modulo(value, size):
    assert size & (size - 1) == 0
    return value & (size - 1)


def attend_kernel(
    steps, requests, heads, len_hbm, tokens_hbm, gain_hbm, table_hbm, rel_hbm, w_hbm, k_hbm, v_hbm,
    out_ref, len_ref, tokens_ref, gain_ref, table_ref, rel_ref, w_buf, k_buf, v_buf,
    bias_buf, score_buf, weight_buf, start_buf, step_buf, small_sem, w_sem, k_sem, v_sem,
):
    tokens = steps * requests
    group = steps * heads
    rows = requests * group
    buckets = rel_ref.shape[1]
    cache_rows, features = k_buf.shape[1:]
    small = (
        (len_hbm, len_ref),
        (table_hbm, table_ref.at[0]),
        (rel_hbm, rel_ref),
        (tokens_hbm, tokens_ref),
        (gain_hbm, gain_ref.at[0]),
    )
    small_copies = [pltpu.make_async_copy(src, dst, small_sem.at[i]) for i, (src, dst) in enumerate(small)]
    w_copies = [pltpu.make_async_copy(w_hbm.at[k], w_buf.at[k], w_sem.at[k]) for k in range(3)]
    per_copy = requests // k_sem.shape[0]
    blocks = [pl.ds(i * per_copy, per_copy) for i in range(k_sem.shape[0])]
    k_copies = [pltpu.make_async_copy(k_hbm.at[b], k_buf.at[b], k_sem.at[i]) for i, b in enumerate(blocks)]
    v_copies = [pltpu.make_async_copy(v_hbm.at[b], v_buf.at[b], v_sem.at[i]) for i, b in enumerate(blocks)]
    for copy in small_copies + w_copies:
        copy.start()

    seq = lax.axis_index("seq")
    base = seq * cache_rows

    for copy in small_copies[:3]:
        copy.wait()
    table = table_ref[...]
    below = jnp.where(table < iota((buckets, table.shape[1]), 0), 1.0, 0.0)
    starts = jnp.sum(below, axis=1, keepdims=True).astype(jnp.int32)
    start_buf[...] = jnp.broadcast_to(starts, (buckets, LANES))

    group_head = over(iota((group, 1), 0), steps)
    level = jnp.zeros((group, buckets), F32)
    for h in range(heads):
        level = jnp.where(group_head == h, rel_ref[h : h + 1, :], level)
    for b in range(buckets):
        step_buf[b] = jnp.broadcast_to(level[:, b : b + 1], (group, LANES))

    def bias_of(pieces):
        width = pieces[0].shape[1]
        biases = [step_buf[0][:, :width]] * len(pieces)
        for b in range(1, buckets):
            start, value = start_buf[b : b + 1, :width], step_buf[b][:, :width]
            biases = [jnp.where(piece >= start, value, bias) for piece, bias in zip(pieces, biases)]
        return biases

    group_step = modulo(iota((group, 1), 0), steps)
    col_slices = [slice(c, c + LANES) for c in range(0, cache_rows, LANES)]
    offsets = [group_step - iota((1, LANES), 1) - (base + c.start) for c in col_slices]
    per_trip = 2

    def fill_bias(trip, carry):
        places, distances = [], []
        for i in range(per_trip):
            r = trip * per_trip + i
            length = len_ref[r]
            for cols, offset in zip(col_slices, offsets):
                places.append((pl.ds(pl.multiple_of(r * group, group), group), cols))
                distances.append(offset + length)
        for place, distance, bias in zip(places, distances, bias_of(distances)):
            bias_buf[place] = jnp.where(distance > group_step, bias, NEG)
        return carry

    for copy in k_copies:
        copy.start()
    lax.fori_loop(0, requests // per_trip, fill_bias, 0)
    for copy in v_copies:
        copy.start()

    for copy in small_copies[3:]:
        copy.wait()
    x = tokens_ref[...].astype(F32)
    normed = rms_scale(x, gain_ref[...]).astype(BF16)
    projected = []
    for copy in w_copies:
        copy.wait()
    for k in range(3):
        projected.append(dot(normed, w_buf[k]).astype(BF16))
    queries, fresh_keys, fresh_values = projected

    row = iota((rows, 1), 0)
    row_step, row_head, row_request = modulo(row, steps), modulo(over(row, steps), heads), over(row, group)
    column = iota((1, tokens), 1)
    pick = jnp.where(row_step * requests + row_request == column, 1.0, 0.0).astype(BF16)
    own_head = row_head == over(iota((1, features), 1), HEAD_DIM)
    spread = jnp.where(own_head, dot(pick, queries), 0.0).astype(BF16)

    key_step, key_request = over(column, requests), modulo(column, requests)
    newest = jnp.where(seq == 0, row_step, -1)
    fresh_live = jnp.logical_and(key_step <= newest, key_request == row_request)
    (fresh_bias,) = bias_of([group_step - key_step])
    fresh_bias = jnp.concatenate([fresh_bias] * requests, axis=0)
    fresh_scores = jnp.where(fresh_live, dot_nt(spread, fresh_keys) + fresh_bias, NEG)

    for copy in k_copies:
        copy.wait()
    for r in range(requests):
        at = slice(r * group, (r + 1) * group)
        score_buf[at, :] = dot_nt(spread[at], k_buf[r])
    scores = score_buf[...] + bias_buf[...]
    top = jnp.maximum(jnp.max(scores, axis=1, keepdims=True), jnp.max(fresh_scores, axis=1, keepdims=True))
    weights = jnp.where(scores > 0.5 * NEG, jnp.exp(scores - top), 0.0)
    fresh_weights = jnp.where(fresh_live, jnp.exp(fresh_scores - top), 0.0)
    total = jnp.sum(weights, axis=1, keepdims=True) + jnp.sum(fresh_weights, axis=1, keepdims=True)
    weight_buf[...] = weights.astype(BF16)
    score_buf[...] = dot(fresh_weights.astype(BF16), fresh_values)
    for copy in v_copies:
        copy.wait()

    lane = iota((1, LANES), 1)
    stats = jnp.where(lane == row_head, top, jnp.where(lane == heads + row_head, total, 0.0))
    group_own = own_head[:group]
    first = iota((8, 1), 0) < steps

    def folded(part):
        half = part[:8] + part[8:]
        return half + pltpu.roll(half, steps, 0)

    stat_pairs = []
    for pair in range(requests // 2):
        sums, stat_parts = [], []
        for r in (2 * pair, 2 * pair + 1):
            at = slice(r * group, (r + 1) * group)
            sums.append(folded(jnp.where(group_own, dot(weight_buf[at, :], v_buf[r]) + score_buf[at, :], 0.0)))
            stat_parts.append(folded(stats[at]))
        out_ref[8 * pair : 8 * pair + 8, :] = jnp.where(first, sums[0], sums[1])
        stat_pairs.append(jnp.where(first, stat_parts[0], stat_parts[1]))
    out_ref[tokens:, :] = jnp.zeros((2 * heads, features), F32)
    out_ref[tokens:, :LANES] = turned(jnp.concatenate(stat_pairs, axis=0))[: 2 * heads]


def turned(value):
    rows = value.shape[0]
    if rows < LANES:
        value = jnp.concatenate([value, jnp.zeros((LANES - rows, LANES), F32)], axis=0)
    return value.T


def widen(columns, first, heads):
    lane_head = over(iota((1, heads * HEAD_DIM), 1), HEAD_DIM)
    wide = jnp.broadcast_to(columns[:, first : first + 1], (columns.shape[0], heads * HEAD_DIM))
    for h in range(1, heads):
        wide = jnp.where(lane_head == h, columns[:, first + h : first + h + 1], wide)
    return wide


def tree(operation, values):
    while len(values) > 1:
        values = [operation(*values[i : i + 2]) for i in range(0, len(values), 2)]
    return values[0]


def merge_parts(tokens, parts):
    heads = parts[0].shape[1] // HEAD_DIM
    stats = [part[tokens:, :LANES] for part in parts]
    top = tree(jnp.maximum, stats)
    scales = [jnp.exp(stat - top) for stat in stats]
    totals = tree(jnp.add, [stat * pltpu.roll(scale, heads, 0) for stat, scale in zip(stats, scales)])
    stat = jnp.where(iota((2 * heads, 1), 0) < heads, top, totals)
    columns = turned(jnp.concatenate(scales + [stat], axis=0))[:tokens]
    sums = tree(
        jnp.add, [part[:tokens, :] * widen(columns, 2 * heads * i, heads) for i, part in enumerate(parts)]
    )
    return sums, stat, widen(columns, 2 * heads * len(parts) + heads, heads)


def merge_kernel(tokens, one_ref, two_ref, _, out_ref):
    sums, stat, _ = merge_parts(tokens, (one_ref, two_ref))
    out_ref[:tokens, :] = sums
    out_ref[tokens:, :] = jnp.zeros((stat.shape[0], sums.shape[1]), F32)
    out_ref[tokens:, :LANES] = stat


def store_halves(value, bit, keep_ref, give_ref):
    half = value.shape[0] // 2
    low = lax.axis_index("tp") // bit % 2 == 0
    keep_ref[...] = jnp.where(low, value[:half], value[half:])
    give_ref[...] = jnp.where(low, value[half:], value[:half])


def project_kernel(steps, requests, one_ref, two_ref, w_ref, _, keep_ref, give_ref):
    tokens = steps * requests
    sums, _, totals = merge_parts(tokens, (one_ref, two_ref))
    attended = (sums / totals).astype(BF16)
    row = iota((tokens, 1), 0)
    source = modulo(row, requests) * steps + over(row, requests)
    order = jnp.where(source == iota((1, tokens), 1), 1.0, 0.0).astype(BF16)
    attended = dot(order, attended).astype(BF16)
    store_halves(dot(attended, w_ref[...]), 1, keep_ref, give_ref)


def chunks_of(total, size):
    return [(at, min(size, total - at)) for at in range(0, total, size)]


def add_kernel(one_ref, two_ref, _, out_ref):
    out_ref[...] = one_ref[...] + two_ref[...]


def fetch_kernel(index, after_ref, weights_hbm, out_ref, done_ref, sems):
    del after_ref
    source = weights_hbm if index is None else weights_hbm.at[index]
    copies = []
    for i, (at, size) in enumerate(chunks_of(out_ref.shape[0], 384)):
        rows = pl.ds(at, size)
        copies.append(pltpu.make_async_copy(source.at[rows], out_ref.at[rows], sems.at[i]))
        copies[-1].start()
    done_ref[...] = jnp.zeros_like(done_ref)
    for copy in copies:
        copy.wait()


def fetch(after, weights, index=None):
    shape = weights.shape[-2:]
    return call(
        functools.partial(fetch_kernel, index),
        [(shape, BF16), ((8, LANES), F32)],
        [VMEM, HBM],
        1,
        [pltpu.SemaphoreType.DMA((len(chunks_of(shape[0], 384)),))],
    )(after, in_hbm(weights))


def own_half_kernel(half_ref, tokens_ref, gain_ref, choice_ref, mid_ref, moe_ref, picks_ref):
    half = half_ref.shape[0]
    steps, _, requests = choice_ref.shape
    low = lax.axis_index("tp") % 2 == 0
    tokens = jnp.where(low, tokens_ref[:half].astype(F32), tokens_ref[half:].astype(F32))
    mid_ref[...] = tokens + half_ref[...]
    moe_ref[...] = rms_scale(mid_ref[...], gain_ref[...]).astype(BF16)
    own = iota((requests, 1), 0) == iota((1, requests), 1)
    lane = iota((1, LANES), 1)
    for t in range(steps):
        columns = [
            jnp.sum(jnp.where(own, choice_ref[t, pick : pick + 1, :].astype(F32), 0.0), axis=1, keepdims=True)
            for pick in range(2)
        ]
        picks_ref[t * requests : (t + 1) * requests, :] = jnp.where(lane == 0, columns[0], columns[1])


def expert_kernel(
    mid_own_ref, moe_own_ref, picks_ref, back_ref, tokens_ref, gain_ref, router_ref, gate_ref, up_ref, down_ref,
    mid_ref, hidden_ref, keep_ref, give_ref,
):
    hidden_local = down_ref.shape[0]
    half = back_ref.shape[0]
    low = lax.axis_index("tp") % 2 == 0
    mid_own, moe_own = mid_own_ref[...], moe_own_ref[...]
    tokens = jnp.where(low, tokens_ref[half:].astype(F32), tokens_ref[:half].astype(F32))
    mid_other = tokens + back_ref[...]
    moe_other = rms_scale(mid_other, gain_ref[...]).astype(BF16)
    mid_ref[:half] = jnp.where(low, mid_own, mid_other)
    mid_ref[half:] = jnp.where(low, mid_other, mid_own)
    moe_in = jnp.concatenate([jnp.where(low, moe_own, moe_other), jnp.where(low, moe_other, moe_own)], axis=0)
    logits = dot_nt(moe_in, router_ref[...])
    expert = iota((1, logits.shape[1]), 1)
    choices = [picks_ref[:, pick : pick + 1].astype(jnp.int32) for pick in range(2)]
    chosen = [jnp.sum(jnp.where(expert == choice, logits, 0.0), axis=1, keepdims=True) for choice in choices]
    first = 1.0 / (1.0 + jnp.exp(chosen[1] - chosen[0]))
    second = 1.0 - first
    device = lax.axis_index("seq") * lax.axis_size("tp") + lax.axis_index("tp")
    column_expert = (device * hidden_local + iota((1, hidden_local), 1)) // FF
    coef = jnp.where(column_expert == choices[0], first, jnp.where(column_expert == choices[1], second, 0.0))
    gate = dot_nt(moe_in, gate_ref[...])
    up = dot_nt(moe_in, up_ref[...])
    hidden = (jax.nn.gelu(gate, approximate=True) * up * coef).astype(BF16)
    hidden_ref[...] = hidden
    store_halves(dot(hidden, down_ref[:, : keep_ref.shape[1]]), 1, keep_ref, give_ref)


def down_kernel(hidden_ref, down_ref, keep_ref, give_ref):
    store_halves(dot(hidden_ref[...], down_ref[:, keep_ref.shape[1] :]), 1, keep_ref, give_ref)


def device_bits(axis):
    size = lax.axis_size(axis)
    assert size & (size - 1) == 0
    return [(axis, 1 << k) for k in range(size.bit_length() - 1)]


def swap(value, bit):
    axis, flip = bit
    return lax.ppermute(value, axis, [(i, i ^ flip) for i in range(lax.axis_size(axis))])


def reduce_columns(halves, split, orders):
    for bits in zip(*orders):
        halves = [half + swap(half, bit) for half, bit in zip(halves, bits)]
    return halves, [swap(half, split) for half in halves]


def in_hbm(value):
    return pltpu.with_memory_space_constraint(value, pltpu.HBM)


def call(kernel, out_shape, in_specs, limit, scratch=()):
    shapes = [jax.ShapeDtypeStruct(shape, dtype) for shape, dtype in out_shape]
    return pl.pallas_call(
        kernel,
        out_shape=shapes,
        in_specs=in_specs,
        out_specs=[VMEM] * len(shapes),
        scratch_shapes=list(scratch),
        compiler_params=pltpu.CompilerParams(vmem_limit_bytes=limit << 20),
    )


def on_device(
    tokens_in,
    key_cache,
    value_cache,
    cache_len,
    bucket_table,
    rel_bias,
    attn_gain,
    moe_gain,
    w_qkv,
    w_out,
    router,
    expert_choice,
    w_gate_up,
    w_down,
):
    steps, requests, width = tokens_in.shape
    tokens = steps * requests
    half = tokens // 2
    _, cache_rows, features = key_cache.shape
    heads = features // HEAD_DIM
    rows = tokens * heads
    buckets = rel_bias.shape[0]
    hidden_local = w_down.shape[0]
    packed_shape = (tokens + 2 * heads, features)
    flat_in = tokens_in.reshape(tokens, width)
    dma = pltpu.SemaphoreType.DMA

    (packed,) = call(
        functools.partial(attend_kernel, steps, requests, heads),
        [(packed_shape, F32)],
        [HBM] * 8,
        16,
        [
            pltpu.SMEM(cache_len.shape, jnp.int32),
            pltpu.VMEM(flat_in.shape, BF16),
            pltpu.VMEM((1, width), F32),
            pltpu.VMEM((1,) + bucket_table.shape, jnp.int32),
            pltpu.VMEM((heads, buckets), F32),
            pltpu.VMEM(w_qkv.shape, BF16),
            pltpu.VMEM(key_cache.shape, BF16),
            pltpu.VMEM(value_cache.shape, BF16),
            pltpu.VMEM((rows, cache_rows), F32),
            pltpu.VMEM((rows, cache_rows), F32),
            pltpu.VMEM((rows, cache_rows), BF16),
            pltpu.VMEM((buckets, LANES), jnp.int32),
            pltpu.VMEM((buckets, steps * heads, LANES), F32),
            dma((5,)),
            dma((3,)),
            dma((requests // 4,)),
            dma((requests // 4,)),
        ],
    )(*map(in_hbm, (cache_len, flat_in, attn_gain, bucket_table, rel_bias.T, w_qkv, key_cache, value_cache)))

    seq_bits, tp_bits = device_bits("seq"), device_bits("tp")
    staged = []
    token = jnp.zeros((8, LANES), F32)
    for i, bit in enumerate(seq_bits):
        other = swap(packed, bit)
        if i >= len(seq_bits) - 2:
            weights, token = fetch(packed, w_gate_up, len(staged))
            staged.append(weights)
        if i < len(seq_bits) - 1:
            (packed,) = call(functools.partial(merge_kernel, tokens), [(packed_shape, F32)], [VMEM] * 3, 2)(
                packed, other, token
            )
    half_shape = ((half, width), F32)
    keep, give = call(
        functools.partial(project_kernel, steps, requests), [half_shape, half_shape], [VMEM] * 4, 4
    )(packed, other, w_out, token)

    half_sum = keep + swap(give, tp_bits[0])
    for bit in tp_bits[1:]:
        other = swap(half_sum, bit)
        if len(staged) == 2:
            weights, token = fetch(half_sum, w_down)
            staged.append(weights)
        (half_sum,) = call(add_kernel, [half_shape], [VMEM] * 3, 1)(half_sum, other, token)
    other = swap(half_sum, tp_bits[0])
    gain = moe_gain[None]
    own_shapes = [half_shape, ((half, width), BF16), ((tokens, LANES), F32)]
    mid_own, moe_own, picks = call(own_half_kernel, own_shapes, [VMEM] * 4, 2)(
        half_sum, flat_in, gain, expert_choice.transpose(0, 2, 1)
    )

    column_shape = ((half, width // 2), F32)
    expert_shapes = [((tokens, width), F32), ((tokens, hidden_local), BF16), column_shape, column_shape]
    mid, hidden, keep, give = call(expert_kernel, expert_shapes, [VMEM] * 10, 8)(
        mid_own, moe_own, picks, other, flat_in, gain, router.T, *staged
    )
    back = swap(give, tp_bits[0])
    keep_two, give_two = call(down_kernel, [column_shape] * 2, [VMEM] * 2, 4)(hidden, staged[2])
    blocks = [keep + back, keep_two + swap(give_two, tp_bits[0])]
    bits = tp_bits[1:] + seq_bits
    swapped = [bits[i ^ 1] if i ^ 1 < len(bits) else bits[i] for i in range(len(bits))]
    mine, other = reduce_columns(blocks, tp_bits[0], (bits, swapped))
    low = lax.axis_index("tp") % 2 == 0
    mine, other = jnp.concatenate(mine, axis=1), jnp.concatenate(other, axis=1)
    mixture = jnp.concatenate([jnp.where(low, mine, other), jnp.where(low, other, mine)])
    return (mid + mixture).astype(BF16).reshape(steps, requests, width)


def solution(mesh):
    return jax.shard_map(
        on_device,
        mesh=mesh,
        in_specs=(
            P(),
            P(None, "seq", "tp"),
            P(None, "seq", "tp"),
            P(),
            P(),
            P(None, "tp"),
            P(),
            P(),
            P(None, None, "tp"),
            P("tp", None),
            P(),
            P(),
            P(None, ("seq", "tp"), None),
            P(("seq", "tp"), None),
        ),
        out_specs=P(),
        check_vma=False,
    )
```

```python
import functools

import jax
import jax.numpy as jnp
from jax import lax
from jax.experimental import pallas as pl
from jax.experimental.pallas import tpu as pltpu
from jax.sharding import PartitionSpec as P

HEAD_DIM = 64
FF = 2816
LANES = 128
NEG = -1e30
EPS = 1e-06
F32 = jnp.float32
BF16 = jnp.bfloat16
VMEM = pl.BlockSpec(memory_space=pltpu.VMEM)
HBM = pl.BlockSpec(memory_space=pltpu.HBM)
NT = (((1,), (1,)), ((), ()))


def dot(one, two):
    return jnp.dot(one, two, preferred_element_type=F32)


def dot_nt(one, two):
    return lax.dot_general(one, two, NT, preferred_element_type=F32)


def iota(shape, dim):
    return lax.broadcasted_iota(jnp.int32, shape, dim)


def rms_scale(values, gain_vec):
    return values * lax.rsqrt(jnp.mean(values * values, axis=-1, keepdims=True) + EPS) * gain_vec


def shift_of(size):
    assert size & (size - 1) == 0
    return size.bit_length() - 1


def over(value, size):
    return lax.shift_right_logical(value, jnp.int32(shift_of(size)))


def modulo(value, size):
    assert size & (size - 1) == 0
    return value & (size - 1)


def attend_kernel(
    steps, requests, heads, len_hbm, tokens_hbm, gain_hbm, table_hbm, rel_hbm, w_hbm, k_hbm, v_hbm,
    out_ref, len_ref, tokens_ref, gain_ref, table_ref, rel_ref, w_buf, k_buf, v_buf,
    bias_buf, score_buf, weight_buf, lane_buf, start_buf, step_buf, small_sem, w_sem, k_sem, v_sem,
):
    tokens = steps * requests
    group = steps * heads
    rows = requests * group
    buckets = rel_ref.shape[1]
    cache_rows, features = k_buf.shape[1:]
    small = (
        (len_hbm, len_ref),
        (table_hbm, table_ref.at[0]),
        (rel_hbm, rel_ref),
        (tokens_hbm, tokens_ref),
        (gain_hbm, gain_ref.at[0]),
    )
    small_copies = [pltpu.make_async_copy(src, dst, small_sem.at[i]) for i, (src, dst) in enumerate(small)]
    w_copies = [pltpu.make_async_copy(w_hbm.at[k], w_buf.at[k], w_sem.at[k]) for k in range(3)]
    per_copy = requests // k_sem.shape[0]
    blocks = [pl.ds(i * per_copy, per_copy) for i in range(k_sem.shape[0])]
    k_copies = [pltpu.make_async_copy(k_hbm.at[b], k_buf.at[b], k_sem.at[i]) for i, b in enumerate(blocks)]
    v_copies = [pltpu.make_async_copy(v_hbm.at[b], v_buf.at[b], v_sem.at[i]) for i, b in enumerate(blocks)]
    for copy in small_copies + w_copies:
        copy.start()

    seq = lax.axis_index("seq")
    base = seq * cache_rows

    for copy in small_copies[:3]:
        copy.wait()
    table = table_ref[...]
    below = jnp.where(table < iota((buckets, table.shape[1]), 0), 1.0, 0.0)
    starts = jnp.sum(below, axis=1, keepdims=True).astype(jnp.int32)
    start_buf[...] = jnp.broadcast_to(starts, (buckets, LANES))

    group_head = over(iota((group, 1), 0), steps)
    level = jnp.zeros((group, buckets), F32)
    for h in range(heads):
        level = jnp.where(group_head == h, rel_ref[h : h + 1, :], level)
    for b in range(buckets):
        step_buf[b] = jnp.broadcast_to(level[:, b : b + 1], (group, LANES))

    def bias_of(pieces):
        width = pieces[0].shape[1]
        biases = [step_buf[0][:, :width]] * len(pieces)
        for b in range(1, buckets):
            start, value = start_buf[b : b + 1, :width], step_buf[b][:, :width]
            biases = [jnp.where(piece >= start, value, bias) for piece, bias in zip(pieces, biases)]
        return biases

    group_step = modulo(iota((group, 1), 0), steps)
    col_slices = [slice(c, c + LANES) for c in range(0, cache_rows, LANES)]
    offsets = [group_step - iota((1, LANES), 1) - (base + c.start) for c in col_slices]
    per_trip = 2

    def fill_bias(trip, carry):
        places, distances = [], []
        for i in range(per_trip):
            r = trip * per_trip + i
            length = len_ref[r]
            for cols, offset in zip(col_slices, offsets):
                places.append((pl.ds(pl.multiple_of(r * group, group), group), cols))
                distances.append(offset + length)
        for place, distance, bias in zip(places, distances, bias_of(distances)):
            bias_buf[place] = jnp.where(distance > group_step, bias, NEG)
        return carry

    for copy in k_copies:
        copy.start()
    lax.fori_loop(0, requests // per_trip, fill_bias, 0)
    for copy in v_copies:
        copy.start()

    for copy in small_copies[3:]:
        copy.wait()
    x = tokens_ref[...].astype(F32)
    normed = rms_scale(x, gain_ref[...]).astype(BF16)
    projected = []
    for copy in w_copies:
        copy.wait()
    for k in range(3):
        projected.append(dot(normed, w_buf[k]).astype(BF16))
    queries, fresh_keys, fresh_values = projected

    row = iota((rows, 1), 0)
    row_step, row_head, row_request = modulo(row, steps), modulo(over(row, steps), heads), over(row, group)
    column = iota((1, tokens), 1)
    pick = jnp.where(row_step * requests + row_request == column, 1.0, 0.0).astype(BF16)
    own_head = row_head == over(iota((1, features), 1), HEAD_DIM)
    spread = jnp.where(own_head, dot(pick, queries), 0.0).astype(BF16)

    key_step, key_request = over(column, requests), modulo(column, requests)
    newest = jnp.where(seq == 0, row_step, -1)
    fresh_live = jnp.logical_and(key_step <= newest, key_request == row_request)
    (fresh_bias,) = bias_of([group_step - key_step])
    fresh_bias = jnp.concatenate([fresh_bias] * requests, axis=0)
    fresh_scores = jnp.where(fresh_live, dot_nt(spread, fresh_keys) + fresh_bias, NEG)

    for copy in k_copies:
        copy.wait()
    for r in range(requests):
        at = slice(r * group, (r + 1) * group)
        score_buf[at, :] = dot_nt(spread[at], k_buf[r])
    scores = score_buf[...] + bias_buf[...]
    top = jnp.maximum(jnp.max(scores, axis=1, keepdims=True), jnp.max(fresh_scores, axis=1, keepdims=True))
    weights = jnp.where(scores > 0.5 * NEG, jnp.exp(scores - top), 0.0)
    fresh_weights = jnp.where(fresh_live, jnp.exp(fresh_scores - top), 0.0)
    total = jnp.sum(weights, axis=1, keepdims=True) + jnp.sum(fresh_weights, axis=1, keepdims=True)
    weight_buf[...] = weights.astype(BF16)
    score_buf[...] = dot(fresh_weights.astype(BF16), fresh_values)
    for copy in v_copies:
        copy.wait()

    lane = iota((1, LANES), 1)
    stats = jnp.where(lane == row_head, top, jnp.where(lane == heads + row_head, total, 0.0))
    group_own = own_head[:group]

    def folded(part):
        half = part[:8] + part[8:]
        return half + pltpu.roll(half, steps, 0)

    blocks_of_lanes = features // LANES
    for r in range(requests):
        at, rows_of = slice(r * group, (r + 1) * group), pl.ds(r, steps, requests)
        own = jnp.where(group_own, dot(weight_buf[at, :], v_buf[r]) + score_buf[at, :], 0.0)
        own = folded(own)[:steps]
        for c in range(blocks_of_lanes):
            lane_buf[c, rows_of, :] = own[:, c * LANES : (c + 1) * LANES]
        lane_buf[blocks_of_lanes, rows_of, :] = folded(stats[at])[:steps]
    for c in range(blocks_of_lanes):
        out_ref[:tokens, c * LANES : (c + 1) * LANES] = lane_buf[c]
    out_ref[tokens:, :] = jnp.zeros((2 * heads, features), F32)
    out_ref[tokens:, :LANES] = turned(lane_buf[blocks_of_lanes])[: 2 * heads]


def turned(value):
    rows = value.shape[0]
    if rows < LANES:
        value = jnp.concatenate([value, jnp.zeros((LANES - rows, LANES), F32)], axis=0)
    return value.T


def widen(columns, first, heads):
    lane_head = over(iota((1, heads * HEAD_DIM), 1), HEAD_DIM)
    wide = jnp.broadcast_to(columns[:, first : first + 1], (columns.shape[0], heads * HEAD_DIM))
    for h in range(1, heads):
        wide = jnp.where(lane_head == h, columns[:, first + h : first + h + 1], wide)
    return wide


def tree(operation, values):
    while len(values) > 1:
        values = [operation(*values[i : i + 2]) for i in range(0, len(values), 2)]
    return values[0]


def merge_parts(tokens, parts):
    heads = parts[0].shape[1] // HEAD_DIM
    stats = [part[tokens:, :LANES] for part in parts]
    top = tree(jnp.maximum, stats)
    scales = [jnp.exp(stat - top) for stat in stats]
    totals = tree(jnp.add, [stat * pltpu.roll(scale, heads, 0) for stat, scale in zip(stats, scales)])
    stat = jnp.where(iota((2 * heads, 1), 0) < heads, top, totals)
    columns = turned(jnp.concatenate(scales + [stat], axis=0))[:tokens]
    sums = tree(
        jnp.add, [part[:tokens, :] * widen(columns, 2 * heads * i, heads) for i, part in enumerate(parts)]
    )
    return sums, stat, widen(columns, 2 * heads * len(parts) + heads, heads)


def merge_kernel(tokens, one_ref, two_ref, _, out_ref):
    sums, stat, _ = merge_parts(tokens, (one_ref, two_ref))
    out_ref[:tokens, :] = sums
    out_ref[tokens:, :] = jnp.zeros((stat.shape[0], sums.shape[1]), F32)
    out_ref[tokens:, :LANES] = stat


def store_halves(value, bit, keep_ref, give_ref):
    half = value.shape[0] // 2
    low = lax.axis_index("tp") // bit % 2 == 0
    keep_ref[...] = jnp.where(low, value[:half], value[half:])
    give_ref[...] = jnp.where(low, value[half:], value[:half])


def project_kernel(tokens, one_ref, two_ref, w_ref, _, keep_ref, give_ref):
    sums, _, totals = merge_parts(tokens, (one_ref, two_ref))
    attended = (sums / totals).astype(BF16)
    store_halves(dot(attended, w_ref[...]), 1, keep_ref, give_ref)


def chunks_of(total, size):
    return [(at, min(size, total - at)) for at in range(0, total, size)]


def add_kernel(one_ref, two_ref, _, out_ref):
    out_ref[...] = one_ref[...] + two_ref[...]


def fetch_kernel(index, after_ref, weights_hbm, out_ref, done_ref, sems):
    del after_ref
    source = weights_hbm if index is None else weights_hbm.at[index]
    copies = []
    for i, (at, size) in enumerate(chunks_of(out_ref.shape[0], 384)):
        rows = pl.ds(at, size)
        copies.append(pltpu.make_async_copy(source.at[rows], out_ref.at[rows], sems.at[i]))
        copies[-1].start()
    done_ref[...] = jnp.zeros_like(done_ref)
    for copy in copies:
        copy.wait()


def fetch(after, weights, index=None):
    shape = weights.shape[-2:]
    return call(
        functools.partial(fetch_kernel, index),
        [(shape, BF16), ((8, LANES), F32)],
        [VMEM, HBM],
        1,
        [pltpu.SemaphoreType.DMA((len(chunks_of(shape[0], 384)),))],
    )(after, in_hbm(weights))


def own_half_kernel(half_ref, tokens_ref, gain_ref, choice_ref, mid_ref, moe_ref, picks_ref):
    half = half_ref.shape[0]
    steps, _, requests = choice_ref.shape
    low = lax.axis_index("tp") % 2 == 0
    tokens = jnp.where(low, tokens_ref[:half].astype(F32), tokens_ref[half:].astype(F32))
    mid_ref[...] = tokens + half_ref[...]
    moe_ref[...] = rms_scale(mid_ref[...], gain_ref[...]).astype(BF16)
    own = iota((requests, 1), 0) == iota((1, requests), 1)
    lane = iota((1, LANES), 1)
    for t in range(steps):
        columns = [
            jnp.sum(jnp.where(own, choice_ref[t, pick : pick + 1, :].astype(F32), 0.0), axis=1, keepdims=True)
            for pick in range(2)
        ]
        picks_ref[t * requests : (t + 1) * requests, :] = jnp.where(lane == 0, columns[0], columns[1])


def expert_kernel(
    mid_own_ref, moe_own_ref, picks_ref, back_ref, tokens_ref, gain_ref, router_ref, gate_ref, up_ref, down_ref,
    mid_ref, hidden_ref, keep_ref, give_ref,
):
    hidden_local = down_ref.shape[0]
    half = back_ref.shape[0]
    low = lax.axis_index("tp") % 2 == 0
    mid_own, moe_own = mid_own_ref[...], moe_own_ref[...]
    tokens = jnp.where(low, tokens_ref[half:].astype(F32), tokens_ref[:half].astype(F32))
    mid_other = tokens + back_ref[...]
    moe_other = rms_scale(mid_other, gain_ref[...]).astype(BF16)
    mid_ref[:half] = jnp.where(low, mid_own, mid_other)
    mid_ref[half:] = jnp.where(low, mid_other, mid_own)
    moe_in = jnp.concatenate([jnp.where(low, moe_own, moe_other), jnp.where(low, moe_other, moe_own)], axis=0)
    logits = dot_nt(moe_in, router_ref[...])
    expert = iota((1, logits.shape[1]), 1)
    choices = [picks_ref[:, pick : pick + 1].astype(jnp.int32) for pick in range(2)]
    chosen = [jnp.sum(jnp.where(expert == choice, logits, 0.0), axis=1, keepdims=True) for choice in choices]
    first = 1.0 / (1.0 + jnp.exp(chosen[1] - chosen[0]))
    second = 1.0 - first
    device = lax.axis_index("seq") * lax.axis_size("tp") + lax.axis_index("tp")
    column_expert = (device * hidden_local + iota((1, hidden_local), 1)) // FF
    coef = jnp.where(column_expert == choices[0], first, jnp.where(column_expert == choices[1], second, 0.0))
    gate = dot_nt(moe_in, gate_ref[...])
    up = dot_nt(moe_in, up_ref[...])
    hidden = (jax.nn.gelu(gate, approximate=True) * up * coef).astype(BF16)
    hidden_ref[...] = hidden
    store_halves(dot(hidden, down_ref[:, : keep_ref.shape[1]]), 1, keep_ref, give_ref)


def down_kernel(hidden_ref, down_ref, keep_ref, give_ref):
    store_halves(dot(hidden_ref[...], down_ref[:, keep_ref.shape[1] :]), 1, keep_ref, give_ref)


def device_bits(axis):
    size = lax.axis_size(axis)
    assert size & (size - 1) == 0
    return [(axis, 1 << k) for k in range(size.bit_length() - 1)]


def swap(value, bit):
    axis, flip = bit
    return lax.ppermute(value, axis, [(i, i ^ flip) for i in range(lax.axis_size(axis))])


def reduce_columns(halves, split, orders):
    for bits in zip(*orders):
        halves = [half + swap(half, bit) for half, bit in zip(halves, bits)]
    return halves, [swap(half, split) for half in halves]


def in_hbm(value):
    return pltpu.with_memory_space_constraint(value, pltpu.HBM)


def call(kernel, out_shape, in_specs, limit, scratch=()):
    shapes = [jax.ShapeDtypeStruct(shape, dtype) for shape, dtype in out_shape]
    return pl.pallas_call(
        kernel,
        out_shape=shapes,
        in_specs=in_specs,
        out_specs=[VMEM] * len(shapes),
        scratch_shapes=list(scratch),
        compiler_params=pltpu.CompilerParams(vmem_limit_bytes=limit << 20),
    )


def on_device(
    tokens_in,
    key_cache,
    value_cache,
    cache_len,
    bucket_table,
    rel_bias,
    attn_gain,
    moe_gain,
    w_qkv,
    w_out,
    router,
    expert_choice,
    w_gate_up,
    w_down,
):
    steps, requests, width = tokens_in.shape
    tokens = steps * requests
    half = tokens // 2
    _, cache_rows, features = key_cache.shape
    heads = features // HEAD_DIM
    rows = tokens * heads
    buckets = rel_bias.shape[0]
    hidden_local = w_down.shape[0]
    packed_shape = (tokens + 2 * heads, features)
    flat_in = tokens_in.reshape(tokens, width)
    dma = pltpu.SemaphoreType.DMA

    (packed,) = call(
        functools.partial(attend_kernel, steps, requests, heads),
        [(packed_shape, F32)],
        [HBM] * 8,
        16,
        [
            pltpu.SMEM(cache_len.shape, jnp.int32),
            pltpu.VMEM(flat_in.shape, BF16),
            pltpu.VMEM((1, width), F32),
            pltpu.VMEM((1,) + bucket_table.shape, jnp.int32),
            pltpu.VMEM((heads, buckets), F32),
            pltpu.VMEM(w_qkv.shape, BF16),
            pltpu.VMEM(key_cache.shape, BF16),
            pltpu.VMEM(value_cache.shape, BF16),
            pltpu.VMEM((rows, cache_rows), F32),
            pltpu.VMEM((rows, cache_rows), F32),
            pltpu.VMEM((rows, cache_rows), BF16),
            pltpu.VMEM((features // LANES + 1, tokens, LANES), F32),
            pltpu.VMEM((buckets, LANES), jnp.int32),
            pltpu.VMEM((buckets, steps * heads, LANES), F32),
            dma((5,)),
            dma((3,)),
            dma((requests // 4,)),
            dma((requests // 4,)),
        ],
    )(*map(in_hbm, (cache_len, flat_in, attn_gain, bucket_table, rel_bias.T, w_qkv, key_cache, value_cache)))

    seq_bits, tp_bits = device_bits("seq"), device_bits("tp")
    staged = []
    token = jnp.zeros((8, LANES), F32)
    for i, bit in enumerate(seq_bits):
        other = swap(packed, bit)
        if i >= len(seq_bits) - 2:
            weights, token = fetch(packed, w_gate_up, len(staged))
            staged.append(weights)
        if i < len(seq_bits) - 1:
            (packed,) = call(functools.partial(merge_kernel, tokens), [(packed_shape, F32)], [VMEM] * 3, 2)(
                packed, other, token
            )
    half_shape = ((half, width), F32)
    keep, give = call(
        functools.partial(project_kernel, tokens), [half_shape, half_shape], [VMEM] * 4, 4
    )(packed, other, w_out, token)

    half_sum = keep + swap(give, tp_bits[0])
    for bit in tp_bits[1:]:
        other = swap(half_sum, bit)
        if len(staged) == 2:
            weights, token = fetch(half_sum, w_down)
            staged.append(weights)
        (half_sum,) = call(add_kernel, [half_shape], [VMEM] * 3, 1)(half_sum, other, token)
    other = swap(half_sum, tp_bits[0])
    gain = moe_gain[None]
    own_shapes = [half_shape, ((half, width), BF16), ((tokens, LANES), F32)]
    mid_own, moe_own, picks = call(own_half_kernel, own_shapes, [VMEM] * 4, 2)(
        half_sum, flat_in, gain, expert_choice.transpose(0, 2, 1)
    )

    column_shape = ((half, width // 2), F32)
    expert_shapes = [((tokens, width), F32), ((tokens, hidden_local), BF16), column_shape, column_shape]
    mid, hidden, keep, give = call(expert_kernel, expert_shapes, [VMEM] * 10, 8)(
        mid_own, moe_own, picks, other, flat_in, gain, router.T, *staged
    )
    back = swap(give, tp_bits[0])
    keep_two, give_two = call(down_kernel, [column_shape] * 2, [VMEM] * 2, 4)(hidden, staged[2])
    blocks = [keep + back, keep_two + swap(give_two, tp_bits[0])]
    bits = tp_bits[1:] + seq_bits
    swapped = [bits[i ^ 1] if i ^ 1 < len(bits) else bits[i] for i in range(len(bits))]
    mine, other = reduce_columns(blocks, tp_bits[0], (bits, swapped))
    low = lax.axis_index("tp") % 2 == 0
    mine, other = jnp.concatenate(mine, axis=1), jnp.concatenate(other, axis=1)
    mixture = jnp.concatenate([jnp.where(low, mine, other), jnp.where(low, other, mine)])
    return (mid + mixture).astype(BF16).reshape(steps, requests, width)


def solution(mesh):
    return jax.shard_map(
        on_device,
        mesh=mesh,
        in_specs=(
            P(),
            P(None, "seq", "tp"),
            P(None, "seq", "tp"),
            P(),
            P(),
            P(None, "tp"),
            P(),
            P(),
            P(None, None, "tp"),
            P("tp", None),
            P(),
            P(),
            P(None, ("seq", "tp"), None),
            P(("seq", "tp"), None),
        ),
        out_specs=P(),
        check_vma=False,
    )
```

```python
import functools

import jax
import jax.numpy as jnp
from jax import lax
from jax.experimental import pallas as pl
from jax.experimental.pallas import tpu as pltpu
from jax.sharding import PartitionSpec as P

HEAD_DIM = 64
FF = 2816
LANES = 128
NEG = -1e30
EPS = 1e-06
F32 = jnp.float32
BF16 = jnp.bfloat16
VMEM = pl.BlockSpec(memory_space=pltpu.VMEM)
HBM = pl.BlockSpec(memory_space=pltpu.HBM)
NT = (((1,), (1,)), ((), ()))


def dot(one, two):
    return jnp.dot(one, two, preferred_element_type=F32)


def dot_nt(one, two):
    return lax.dot_general(one, two, NT, preferred_element_type=F32)


def iota(shape, dim):
    return lax.broadcasted_iota(jnp.int32, shape, dim)


def rms_scale(values, gain_vec):
    return values * lax.rsqrt(jnp.mean(values * values, axis=-1, keepdims=True) + EPS) * gain_vec


def shift_of(size):
    assert size & (size - 1) == 0
    return size.bit_length() - 1


def over(value, size):
    return lax.shift_right_logical(value, jnp.int32(shift_of(size)))


def modulo(value, size):
    assert size & (size - 1) == 0
    return value & (size - 1)


def attend_kernel(
    steps, requests, heads, len_hbm, tokens_hbm, gain_hbm, table_hbm, rel_hbm, w_hbm, k_hbm, v_hbm,
    out_ref, len_ref, tokens_ref, gain_ref, table_ref, rel_ref, w_buf, k_buf, v_buf,
    bias_buf, score_buf, weight_buf, lane_buf, start_buf, step_buf, small_sem, w_sem, k_sem, v_sem,
):
    tokens = steps * requests
    group = steps * heads
    rows = requests * group
    buckets = rel_ref.shape[1]
    cache_rows, features = k_buf.shape[1:]
    small = (
        (len_hbm, len_ref),
        (table_hbm, table_ref.at[0]),
        (rel_hbm, rel_ref),
        (tokens_hbm, tokens_ref),
        (gain_hbm, gain_ref.at[0]),
    )
    small_copies = [pltpu.make_async_copy(src, dst, small_sem.at[i]) for i, (src, dst) in enumerate(small)]
    w_copies = [pltpu.make_async_copy(w_hbm.at[k], w_buf.at[k], w_sem.at[k]) for k in range(3)]
    per_copy = requests // k_sem.shape[0]
    blocks = [pl.ds(i * per_copy, per_copy) for i in range(k_sem.shape[0])]
    k_copies = [pltpu.make_async_copy(k_hbm.at[b], k_buf.at[b], k_sem.at[i]) for i, b in enumerate(blocks)]
    v_copies = [pltpu.make_async_copy(v_hbm.at[b], v_buf.at[b], v_sem.at[i]) for i, b in enumerate(blocks)]
    for copy in small_copies + w_copies:
        copy.start()

    seq = lax.axis_index("seq")
    base = seq * cache_rows

    for copy in small_copies[:3]:
        copy.wait()
    table = table_ref[...]
    below = jnp.where(table < iota((buckets, table.shape[1]), 0), 1.0, 0.0)
    starts = jnp.sum(below, axis=1, keepdims=True).astype(jnp.int32)
    start_buf[...] = jnp.broadcast_to(starts, (buckets, LANES))

    group_head = over(iota((group, 1), 0), steps)
    level = jnp.zeros((group, buckets), F32)
    for h in range(heads):
        level = jnp.where(group_head == h, rel_ref[h : h + 1, :], level)
    for b in range(buckets):
        step_buf[b] = jnp.broadcast_to(level[:, b : b + 1], (group, LANES))

    def bias_of(pieces):
        width = pieces[0].shape[1]
        biases = [step_buf[0][:, :width]] * len(pieces)
        for b in range(1, buckets):
            start, value = start_buf[b : b + 1, :width], step_buf[b][:, :width]
            biases = [jnp.where(piece >= start, value, bias) for piece, bias in zip(pieces, biases)]
        return biases

    group_step = modulo(iota((group, 1), 0), steps)
    col_slices = [slice(c, c + LANES) for c in range(0, cache_rows, LANES)]
    offsets = [group_step - iota((1, LANES), 1) - (base + c.start) for c in col_slices]
    per_trip = 2

    def fill_bias(trip, carry):
        places, distances = [], []
        for i in range(per_trip):
            r = trip * per_trip + i
            length = len_ref[r]
            for cols, offset in zip(col_slices, offsets):
                places.append((pl.ds(pl.multiple_of(r * group, group), group), cols))
                distances.append(offset + length)
        for place, distance, bias in zip(places, distances, bias_of(distances)):
            bias_buf[place] = jnp.where(distance > group_step, bias, NEG)
        return carry

    for copy in k_copies:
        copy.start()
    lax.fori_loop(0, requests // per_trip, fill_bias, 0)
    for copy in v_copies:
        copy.start()

    for copy in small_copies[3:]:
        copy.wait()
    x = tokens_ref[...].astype(F32)
    normed = rms_scale(x, gain_ref[...]).astype(BF16)
    projected = []
    for copy in w_copies:
        copy.wait()
    for k in range(3):
        projected.append(dot(normed, w_buf[k]).astype(BF16))
    queries, fresh_keys, fresh_values = projected

    row = iota((rows, 1), 0)
    row_step, row_head, row_request = modulo(row, steps), modulo(over(row, steps), heads), over(row, group)
    column = iota((1, tokens), 1)
    pick = jnp.where(row_step * requests + row_request == column, 1.0, 0.0).astype(BF16)
    own_head = row_head == over(iota((1, features), 1), HEAD_DIM)
    spread = jnp.where(own_head, dot(pick, queries), 0.0).astype(BF16)

    key_step, key_request = over(column, requests), modulo(column, requests)
    newest = jnp.where(seq == 0, row_step, -1)
    fresh_live = jnp.logical_and(key_step <= newest, key_request == row_request)
    (fresh_bias,) = bias_of([group_step - key_step])
    fresh_bias = jnp.concatenate([fresh_bias] * requests, axis=0)
    fresh_scores = jnp.where(fresh_live, dot_nt(spread, fresh_keys) + fresh_bias, NEG)

    for copy in k_copies:
        copy.wait()
    for r in range(requests):
        at = slice(r * group, (r + 1) * group)
        score_buf[at, :] = dot_nt(spread[at], k_buf[r])
    scores = score_buf[...] + bias_buf[...]
    top = jnp.maximum(jnp.max(scores, axis=1, keepdims=True), jnp.max(fresh_scores, axis=1, keepdims=True))
    weights = jnp.where(scores > 0.5 * NEG, jnp.exp(scores - top), 0.0)
    fresh_weights = jnp.where(fresh_live, jnp.exp(fresh_scores - top), 0.0)
    total = jnp.sum(weights, axis=1, keepdims=True) + jnp.sum(fresh_weights, axis=1, keepdims=True)
    weight_buf[...] = weights.astype(BF16)
    fresh_rows = fresh_weights.astype(BF16)
    for copy in v_copies:
        copy.wait()

    lane = iota((1, LANES), 1)
    stats = jnp.where(lane == row_head, top, jnp.where(lane == heads + row_head, total, 0.0))
    group_own = own_head[:group]

    def folded(part):
        half = part[:8] + part[8:]
        return half + pltpu.roll(half, steps, 0)

    blocks_of_lanes = features // LANES
    for r in range(requests):
        at, rows_of = slice(r * group, (r + 1) * group), pl.ds(r, steps, requests)
        own = jnp.where(group_own, dot(weight_buf[at, :], v_buf[r]) + dot(fresh_rows[at], fresh_values), 0.0)
        own = folded(own)[:steps]
        for c in range(blocks_of_lanes):
            lane_buf[c, rows_of, :] = own[:, c * LANES : (c + 1) * LANES]
        lane_buf[blocks_of_lanes, rows_of, :] = folded(stats[at])[:steps]
    for c in range(blocks_of_lanes):
        out_ref[:tokens, c * LANES : (c + 1) * LANES] = lane_buf[c]
    out_ref[tokens:, :] = jnp.zeros((2 * heads, features), F32)
    out_ref[tokens:, :LANES] = turned(lane_buf[blocks_of_lanes])[: 2 * heads]


def turned(value):
    rows = value.shape[0]
    if rows < LANES:
        value = jnp.concatenate([value, jnp.zeros((LANES - rows, LANES), F32)], axis=0)
    return value.T


def widen(columns, first, heads):
    lane_head = over(iota((1, heads * HEAD_DIM), 1), HEAD_DIM)
    wide = jnp.broadcast_to(columns[:, first : first + 1], (columns.shape[0], heads * HEAD_DIM))
    for h in range(1, heads):
        wide = jnp.where(lane_head == h, columns[:, first + h : first + h + 1], wide)
    return wide


def tree(operation, values):
    while len(values) > 1:
        values = [operation(*values[i : i + 2]) for i in range(0, len(values), 2)]
    return values[0]


def merge_parts(tokens, parts):
    heads = parts[0].shape[1] // HEAD_DIM
    stats = [part[tokens:, :LANES] for part in parts]
    top = tree(jnp.maximum, stats)
    scales = [jnp.exp(stat - top) for stat in stats]
    totals = tree(jnp.add, [stat * pltpu.roll(scale, heads, 0) for stat, scale in zip(stats, scales)])
    stat = jnp.where(iota((2 * heads, 1), 0) < heads, top, totals)
    columns = turned(jnp.concatenate(scales + [stat], axis=0))[:tokens]
    sums = tree(
        jnp.add, [part[:tokens, :] * widen(columns, 2 * heads * i, heads) for i, part in enumerate(parts)]
    )
    return sums, stat, widen(columns, 2 * heads * len(parts) + heads, heads)


def merge_kernel(tokens, one_ref, two_ref, _, out_ref):
    sums, stat, _ = merge_parts(tokens, (one_ref, two_ref))
    out_ref[:tokens, :] = sums
    out_ref[tokens:, :] = jnp.zeros((stat.shape[0], sums.shape[1]), F32)
    out_ref[tokens:, :LANES] = stat


def store_halves(value, bit, keep_ref, give_ref):
    half = value.shape[0] // 2
    low = lax.axis_index("tp") // bit % 2 == 0
    keep_ref[...] = jnp.where(low, value[:half], value[half:])
    give_ref[...] = jnp.where(low, value[half:], value[:half])


def project_kernel(tokens, one_ref, two_ref, w_ref, _, keep_ref, give_ref):
    sums, _, totals = merge_parts(tokens, (one_ref, two_ref))
    attended = (sums / totals).astype(BF16)
    store_halves(dot(attended, w_ref[...]), 1, keep_ref, give_ref)


def chunks_of(total, size):
    return [(at, min(size, total - at)) for at in range(0, total, size)]


def add_kernel(one_ref, two_ref, _, out_ref):
    out_ref[...] = one_ref[...] + two_ref[...]


def fetch_kernel(index, after_ref, weights_hbm, out_ref, done_ref, sems):
    del after_ref
    source = weights_hbm if index is None else weights_hbm.at[index]
    copies = []
    for i, (at, size) in enumerate(chunks_of(out_ref.shape[0], 384)):
        rows = pl.ds(at, size)
        copies.append(pltpu.make_async_copy(source.at[rows], out_ref.at[rows], sems.at[i]))
        copies[-1].start()
    done_ref[...] = jnp.zeros_like(done_ref)
    for copy in copies:
        copy.wait()


def fetch(after, weights, index=None):
    shape = weights.shape[-2:]
    return call(
        functools.partial(fetch_kernel, index),
        [(shape, BF16), ((8, LANES), F32)],
        [VMEM, HBM],
        1,
        [pltpu.SemaphoreType.DMA((len(chunks_of(shape[0], 384)),))],
    )(after, in_hbm(weights))


def own_half_kernel(half_ref, tokens_ref, gain_ref, choice_ref, mid_ref, moe_ref, picks_ref):
    half = half_ref.shape[0]
    steps, _, requests = choice_ref.shape
    low = lax.axis_index("tp") % 2 == 0
    tokens = jnp.where(low, tokens_ref[:half].astype(F32), tokens_ref[half:].astype(F32))
    mid_ref[...] = tokens + half_ref[...]
    moe_ref[...] = rms_scale(mid_ref[...], gain_ref[...]).astype(BF16)
    own = iota((requests, 1), 0) == iota((1, requests), 1)
    lane = iota((1, LANES), 1)
    for t in range(steps):
        columns = [
            jnp.sum(jnp.where(own, choice_ref[t, pick : pick + 1, :].astype(F32), 0.0), axis=1, keepdims=True)
            for pick in range(2)
        ]
        picks_ref[t * requests : (t + 1) * requests, :] = jnp.where(lane == 0, columns[0], columns[1])


def expert_kernel(
    mid_own_ref, moe_own_ref, picks_ref, back_ref, tokens_ref, gain_ref, router_ref, gate_ref, up_ref, down_ref,
    mid_ref, hidden_ref, keep_ref, give_ref,
):
    hidden_local = down_ref.shape[0]
    half = back_ref.shape[0]
    low = lax.axis_index("tp") % 2 == 0
    mid_own, moe_own = mid_own_ref[...], moe_own_ref[...]
    tokens = jnp.where(low, tokens_ref[half:].astype(F32), tokens_ref[:half].astype(F32))
    mid_other = tokens + back_ref[...]
    moe_other = rms_scale(mid_other, gain_ref[...]).astype(BF16)
    mid_ref[:half] = jnp.where(low, mid_own, mid_other)
    mid_ref[half:] = jnp.where(low, mid_other, mid_own)
    moe_in = jnp.concatenate([jnp.where(low, moe_own, moe_other), jnp.where(low, moe_other, moe_own)], axis=0)
    logits = dot_nt(moe_in, router_ref[...])
    expert = iota((1, logits.shape[1]), 1)
    choices = [picks_ref[:, pick : pick + 1].astype(jnp.int32) for pick in range(2)]
    chosen = [jnp.sum(jnp.where(expert == choice, logits, 0.0), axis=1, keepdims=True) for choice in choices]
    first = 1.0 / (1.0 + jnp.exp(chosen[1] - chosen[0]))
    second = 1.0 - first
    device = lax.axis_index("seq") * lax.axis_size("tp") + lax.axis_index("tp")
    column_expert = (device * hidden_local + iota((1, hidden_local), 1)) // FF
    coef = jnp.where(column_expert == choices[0], first, jnp.where(column_expert == choices[1], second, 0.0))
    gate = dot_nt(moe_in, gate_ref[...])
    up = dot_nt(moe_in, up_ref[...])
    hidden = (jax.nn.gelu(gate, approximate=True) * up * coef).astype(BF16)
    hidden_ref[...] = hidden
    store_halves(dot(hidden, down_ref[:, : keep_ref.shape[1]]), 1, keep_ref, give_ref)


def down_kernel(hidden_ref, down_ref, keep_ref, give_ref):
    store_halves(dot(hidden_ref[...], down_ref[:, keep_ref.shape[1] :]), 1, keep_ref, give_ref)


def device_bits(axis):
    size = lax.axis_size(axis)
    assert size & (size - 1) == 0
    return [(axis, 1 << k) for k in range(size.bit_length() - 1)]


def swap(value, bit):
    axis, flip = bit
    return lax.ppermute(value, axis, [(i, i ^ flip) for i in range(lax.axis_size(axis))])


def reduce_columns(halves, split, orders):
    for bits in zip(*orders):
        halves = [half + swap(half, bit) for half, bit in zip(halves, bits)]
    return halves, [swap(half, split) for half in halves]


def in_hbm(value):
    return pltpu.with_memory_space_constraint(value, pltpu.HBM)


def call(kernel, out_shape, in_specs, limit, scratch=()):
    shapes = [jax.ShapeDtypeStruct(shape, dtype) for shape, dtype in out_shape]
    return pl.pallas_call(
        kernel,
        out_shape=shapes,
        in_specs=in_specs,
        out_specs=[VMEM] * len(shapes),
        scratch_shapes=list(scratch),
        compiler_params=pltpu.CompilerParams(vmem_limit_bytes=limit << 20),
    )


def on_device(
    tokens_in,
    key_cache,
    value_cache,
    cache_len,
    bucket_table,
    rel_bias,
    attn_gain,
    moe_gain,
    w_qkv,
    w_out,
    router,
    expert_choice,
    w_gate_up,
    w_down,
):
    steps, requests, width = tokens_in.shape
    tokens = steps * requests
    half = tokens // 2
    _, cache_rows, features = key_cache.shape
    heads = features // HEAD_DIM
    rows = tokens * heads
    buckets = rel_bias.shape[0]
    hidden_local = w_down.shape[0]
    packed_shape = (tokens + 2 * heads, features)
    flat_in = tokens_in.reshape(tokens, width)
    dma = pltpu.SemaphoreType.DMA

    (packed,) = call(
        functools.partial(attend_kernel, steps, requests, heads),
        [(packed_shape, F32)],
        [HBM] * 8,
        16,
        [
            pltpu.SMEM(cache_len.shape, jnp.int32),
            pltpu.VMEM(flat_in.shape, BF16),
            pltpu.VMEM((1, width), F32),
            pltpu.VMEM((1,) + bucket_table.shape, jnp.int32),
            pltpu.VMEM((heads, buckets), F32),
            pltpu.VMEM(w_qkv.shape, BF16),
            pltpu.VMEM(key_cache.shape, BF16),
            pltpu.VMEM(value_cache.shape, BF16),
            pltpu.VMEM((rows, cache_rows), F32),
            pltpu.VMEM((rows, cache_rows), F32),
            pltpu.VMEM((rows, cache_rows), BF16),
            pltpu.VMEM((features // LANES + 1, tokens, LANES), F32),
            pltpu.VMEM((buckets, LANES), jnp.int32),
            pltpu.VMEM((buckets, steps * heads, LANES), F32),
            dma((5,)),
            dma((3,)),
            dma((requests // 4,)),
            dma((requests // 4,)),
        ],
    )(*map(in_hbm, (cache_len, flat_in, attn_gain, bucket_table, rel_bias.T, w_qkv, key_cache, value_cache)))

    seq_bits, tp_bits = device_bits("seq"), device_bits("tp")
    staged = []
    token = jnp.zeros((8, LANES), F32)
    for i, bit in enumerate(seq_bits):
        other = swap(packed, bit)
        if i >= len(seq_bits) - 2:
            weights, token = fetch(packed, w_gate_up, len(staged))
            staged.append(weights)
        if i < len(seq_bits) - 1:
            (packed,) = call(functools.partial(merge_kernel, tokens), [(packed_shape, F32)], [VMEM] * 3, 2)(
                packed, other, token
            )
    half_shape = ((half, width), F32)
    keep, give = call(
        functools.partial(project_kernel, tokens), [half_shape, half_shape], [VMEM] * 4, 4
    )(packed, other, w_out, token)

    half_sum = keep + swap(give, tp_bits[0])
    for bit in tp_bits[1:]:
        other = swap(half_sum, bit)
        if len(staged) == 2:
            weights, token = fetch(half_sum, w_down)
            staged.append(weights)
        (half_sum,) = call(add_kernel, [half_shape], [VMEM] * 3, 1)(half_sum, other, token)
    other = swap(half_sum, tp_bits[0])
    gain = moe_gain[None]
    own_shapes = [half_shape, ((half, width), BF16), ((tokens, LANES), F32)]
    mid_own, moe_own, picks = call(own_half_kernel, own_shapes, [VMEM] * 4, 2)(
        half_sum, flat_in, gain, expert_choice.transpose(0, 2, 1)
    )

    column_shape = ((half, width // 2), F32)
    expert_shapes = [((tokens, width), F32), ((tokens, hidden_local), BF16), column_shape, column_shape]
    mid, hidden, keep, give = call(expert_kernel, expert_shapes, [VMEM] * 10, 8)(
        mid_own, moe_own, picks, other, flat_in, gain, router.T, *staged
    )
    back = swap(give, tp_bits[0])
    keep_two, give_two = call(down_kernel, [column_shape] * 2, [VMEM] * 2, 4)(hidden, staged[2])
    blocks = [keep + back, keep_two + swap(give_two, tp_bits[0])]
    bits = tp_bits[1:] + seq_bits
    swapped = [bits[i ^ 1] if i ^ 1 < len(bits) else bits[i] for i in range(len(bits))]
    mine, other = reduce_columns(blocks, tp_bits[0], (bits, swapped))
    low = lax.axis_index("tp") % 2 == 0
    mine, other = jnp.concatenate(mine, axis=1), jnp.concatenate(other, axis=1)
    mixture = jnp.concatenate([jnp.where(low, mine, other), jnp.where(low, other, mine)])
    return (mid + mixture).astype(BF16).reshape(steps, requests, width)


def solution(mesh):
    return jax.shard_map(
        on_device,
        mesh=mesh,
        in_specs=(
            P(),
            P(None, "seq", "tp"),
            P(None, "seq", "tp"),
            P(),
            P(),
            P(None, "tp"),
            P(),
            P(),
            P(None, None, "tp"),
            P("tp", None),
            P(),
            P(),
            P(None, ("seq", "tp"), None),
            P(("seq", "tp"), None),
        ),
        out_specs=P(),
        check_vma=False,
    )
```
